512 devices in a mesh: ta: 8 (over x, z_hi), ha: 8 (over z_lo, core), hd: 8 (over y).
Axes of the slice: x: 4, y: 8, z: 8 (z_hi: 2, z_lo: 4; z = z_hi * 4 + z_lo), core: 2. Of those that a mesh axis runs over, the one named last changes fastest.
Arguments:
- qkv: bfloat16 [32, 32, 64, 9216], P('ta', 'ha', 'hd'), may hold values from -40 to 40, as said below
- q_gain: float32 [128], replicated, may hold values from 0.5 to 4.5
- k_gain: float32 [128], replicated, may hold values from 0.5 to 4.5
- windows: int32 [24, 3], P('hd'), may hold values from 0 to 1, as said below
- frame_counts: int32 [16], replicated, may hold values from 1 to 2, as said below
- row_counts: int32 [16], replicated, may hold values from 1 to 2, as said below
Outputs:
- attended: bfloat16 [32, 32, 64, 3072], P('ta', 'ha', 'hd')
The draws below stay inside these ranges and needn't reach their ends.
Inputs may be any that keep to these rules, and one draw needn't show every extreme that they name: `qkv`: the last dimension holds the query, then the key, then the value, each as 24 heads of 128 entries. `windows`: every column reaches 1 for some head. `frame_counts`: some tile holds 2 frames. `row_counts`: some tile holds 2 rows.
All inputs are finite; a program needn't handle non-finite values.
Results may differ from the reference program's by a relative error of at most 0.012.
The reference program's roundings to bfloat16 on the way (of `weights`) count: a program that leaves them out, or rounds other values in their place, can miss the bound.
Values may be sent and summed in bfloat16 or wider, within the bound.
No kernel may reach another device: no remote copies, remote signals or barrier semaphores. Data moves between devices by JAX's collectives and lax.ppermute only.
A program may use at most 64 MiB of HBM per device.

```python
import math
import jax
import jax.numpy as jnp
from jax import lax

HEADS = 24
HEAD_DIM = 128
TT = 2
TH = 2
TW = 8
COLS = 64
FRAMES = 32
ROWS = 32
TILES_T = 16
TILES_H = 16


def draw_qkv(key, part):
    layout = (FRAMES, ROWS, COLS, 3, HEADS, HEAD_DIM)
    values = jnp.clip(jax.random.normal(jax.random.fold_in(key, 1), layout, jnp.float32), -6.0, 6.0)
    return values.reshape(FRAMES, ROWS, COLS, 3 * HEADS * HEAD_DIM).astype(jnp.bfloat16)


def draw_q_gain(key, part):
    values = jnp.exp(jax.random.uniform(jax.random.fold_in(key, 62), (HEAD_DIM,), jnp.float32, math.log(0.5), math.log(2.0)))
    return values.astype(jnp.float32)


def draw_k_gain(key, part):
    values = jnp.exp(jax.random.uniform(jax.random.fold_in(key, 72), (HEAD_DIM,), jnp.float32, math.log(0.5), math.log(2.0)))
    return values.astype(jnp.float32)


def draw_windows(key, part):
    radius = jax.random.randint(jax.random.fold_in(key, 21), (HEADS, 3), 0, 2)
    forced = jax.random.randint(jax.random.fold_in(key, 22), (1, 3), 0, HEADS)
    return jnp.where(jnp.arange(HEADS)[:, None] == forced, 1, radius).astype(jnp.int32)


def count_tables(key):
    base = jax.random.fold_in(key, 30)
    frames = jax.random.randint(jax.random.fold_in(base, 1), (TILES_T,), 1, TT + 1)
    frame_forced = jax.random.randint(jax.random.fold_in(base, 2), (), 0, TILES_T)
    frames = jnp.where(jnp.arange(TILES_T) == frame_forced, TT, frames)
    rows = jax.random.randint(jax.random.fold_in(base, 3), (TILES_H,), 1, TH + 1)
    spot = jax.random.randint(jax.random.fold_in(base, 4), (), 0, min(TILES_T, TILES_H))
    row_forced = (spot + 1 + jax.random.randint(jax.random.fold_in(base, 5), (), 0, TILES_H - 1)) % TILES_H
    frame_at = jnp.sum(jnp.where(jnp.arange(TILES_T) == spot, frames, 0))
    rows = jnp.where(jnp.arange(TILES_H) == spot, TH + 1 - frame_at, rows)
    rows = jnp.where(jnp.arange(TILES_H) == row_forced, TH, rows)
    return (frames.astype(jnp.int32), rows.astype(jnp.int32))


def draw_frame_counts(key, part):
    return count_tables(key)[0]


def draw_row_counts(key, part):
    return count_tables(key)[1]


def setup_inputs(seed: int = 0) -> dict:
    keys = jax.random.split(jax.random.key(seed), 7)
    qkv = draw_qkv(jax.random.fold_in(keys[6], 71), 0)
    q_gain = draw_q_gain(jax.random.fold_in(keys[6], 71), 0)
    k_gain = draw_k_gain(jax.random.fold_in(keys[6], 71), 0)
    windows = draw_windows(jax.random.fold_in(keys[6], 71), 0)
    frame_counts = draw_frame_counts(jax.random.fold_in(keys[6], 71), 0)
    row_counts = draw_row_counts(jax.random.fold_in(keys[6], 71), 0)
    return dict(qkv=qkv, q_gain=q_gain, k_gain=k_gain, windows=windows, frame_counts=frame_counts, row_counts=row_counts)


def normalize(part_values, gain):
    widened = part_values.astype(jnp.float32)
    meansq = lax.optimization_barrier(jnp.mean(widened * widened, axis=-1, keepdims=True))
    return (widened * lax.rsqrt(meansq + 1e-06) * gain).astype(jnp.bfloat16)

def valid_cells(position, extent, counts):
    tile_index = position // extent
    listed = jnp.arange(counts.shape[0], dtype=jnp.int32)
    holding = lax.optimization_barrier(jnp.sum(jnp.where(tile_index[:, None] == listed[None, :], counts[None, :], 0), axis=1))
    return position % extent < holding

def reference(qkv, q_gain, k_gain, windows, frame_counts, row_counts):
    grouped = qkv.reshape(FRAMES, ROWS, COLS, 3, HEADS, HEAD_DIM)
    queries = normalize(grouped[:, :, :, 0], q_gain)
    widths = ((TT, TT), (TH, TH), (0, 0), (0, 0), (0, 0))
    keys_pad = jnp.pad(normalize(grouped[:, :, :, 1], k_gain), widths)
    values_pad = jnp.pad(grouped[:, :, :, 2], widths)
    col_tiles = jnp.arange(COLS, dtype=jnp.int32) // TW
    col_mask = jnp.abs(col_tiles[None, :, None] - col_tiles[None, None, :]) <= windows[:, 2, None, None]
    score_scale = 1.0 / math.sqrt(HEAD_DIM)

    def one_block(number):
        time_tile = number // TILES_H
        row_tile = number % TILES_H
        frame_start = (time_tile * TT).astype(jnp.int32)
        row_start = (row_tile * TH).astype(jnp.int32)
        zero = jnp.zeros((), jnp.int32)
        query_block = lax.dynamic_slice(queries, (frame_start, row_start, zero, zero, zero), (TT, TH, COLS, HEADS, HEAD_DIM)).reshape(-1, HEADS, HEAD_DIM)
        key_block = lax.dynamic_slice(keys_pad, (frame_start, row_start, zero, zero, zero), (3 * TT, 3 * TH, COLS, HEADS, HEAD_DIM)).reshape(-1, HEADS, HEAD_DIM)
        value_block = lax.dynamic_slice(values_pad, (frame_start, row_start, zero, zero, zero), (3 * TT, 3 * TH, COLS, HEADS, HEAD_DIM)).reshape(-1, HEADS, HEAD_DIM)
        query_frames = frame_start + jnp.arange(TT, dtype=jnp.int32)
        key_frames = frame_start - TT + jnp.arange(3 * TT, dtype=jnp.int32)
        query_rows = row_start + jnp.arange(TH, dtype=jnp.int32)
        key_rows = row_start - TH + jnp.arange(3 * TH, dtype=jnp.int32)
        time_mask = (jnp.abs(query_frames[None, :, None] // TT - key_frames[None, None, :] // TT) <= windows[:, 0, None, None]) & valid_cells(key_frames, TT, frame_counts)[None, None, :]
        row_mask = (jnp.abs(query_rows[None, :, None] // TH - key_rows[None, None, :] // TH) <= windows[:, 1, None, None]) & valid_cells(key_rows, TH, row_counts)[None, None, :]
        allowed = (time_mask[:, :, None, None, :, None, None] & row_mask[:, None, :, None, None, :, None] & col_mask[:, None, None, :, None, None, :]).reshape(HEADS, query_block.shape[0], key_block.shape[0])
        query_live = (valid_cells(query_frames, TT, frame_counts)[:, None, None] & valid_cells(query_rows, TH, row_counts)[None, :, None] & (col_tiles >= 0)[None, None, :]).reshape(-1)
        scores = jnp.einsum('qhd,khd->hqk', query_block.astype(jnp.float32), key_block.astype(jnp.float32)) * score_scale
        scores = jnp.where(allowed, scores, -1e+30)
        highest = lax.optimization_barrier(jnp.max(scores, axis=2, keepdims=True))
        raised = jnp.exp(scores - highest)
        summed = lax.optimization_barrier(jnp.sum(raised, axis=2, keepdims=True))
        weights = raised.astype(jnp.bfloat16)
        blended = jnp.einsum('hqk,khd->qhd', weights.astype(jnp.float32), value_block.astype(jnp.float32))
        result = jnp.where(query_live[:, None, None], blended / summed.transpose(1, 0, 2), 0.0)
        return result.astype(jnp.bfloat16)
    blocks = lax.map(one_block, jnp.arange(TILES_T * TILES_H, dtype=jnp.int32))
    blocks = blocks.reshape(TILES_T, TILES_H, TT, TH, COLS, HEADS, HEAD_DIM)
    return blocks.transpose(0, 2, 1, 3, 4, 5, 6).reshape(FRAMES, ROWS, COLS, HEADS * HEAD_DIM)
```

```python
import functools
import math

import jax
import jax.numpy as jnp
from jax import lax
from jax.experimental import pallas as pl
from jax.experimental.pallas import tpu as pltpu
from jax.sharding import PartitionSpec as P

TT = 2
TH = 2
TW = 8
NEG = -1e30


def normed(x, gain):
    meansq = jnp.mean(x * x, axis=-1, keepdims=True)
    return x * lax.rsqrt(meansq + 1e-06) * gain


def pack_kernel(entries, parts, heads_local, groups, *refs):
    part_refs = refs[: len(parts)]
    qg_ref, kg_ref, out_ref = refs[len(parts) :]
    rows, cols = part_refs[0].shape[1:3]
    head_dim = qg_ref.shape[-1]
    gains = {0: qg_ref[...].reshape(1, 1, head_dim), 1: kg_ref[...].reshape(1, 1, head_dim)}
    for dest in range(groups):
        for slot, (part, head) in enumerate(entries):
            at = (heads_local * dest + head) * head_dim
            x = part_refs[parts.index(part)][0, :, :, at : at + head_dim].astype(jnp.float32)
            if part in gains:
                x = normed(x, gains[part])
            out_ref[dest, slot, 0] = x.reshape(rows * cols, head_dim).astype(jnp.bfloat16)


def pack(qkv, q_gain, k_gain, entries, heads_local, groups):
    frames, rows, cols, channels = qkv.shape
    head_dim = q_gain.shape[-1]
    third = channels // 3
    parts = sorted({part for part, _ in entries})
    n = len(entries)
    gain_spec = pl.BlockSpec((1, head_dim), lambda f: (0, 0))
    return pl.pallas_call(
        functools.partial(pack_kernel, entries, parts, heads_local, groups),
        grid=(frames,),
        in_specs=[
            pl.BlockSpec((1, rows, cols, third), functools.partial(lambda p, f: (f, 0, 0, p), part))
            for part in parts
        ]
        + [gain_spec, gain_spec],
        out_specs=pl.BlockSpec(
            (groups, n, 1, rows * cols, head_dim), lambda f: (0, 0, f, 0, 0)
        ),
        out_shape=jax.ShapeDtypeStruct((groups, n, frames, rows * cols, head_dim), jnp.bfloat16),
        cost_estimate=pl.CostEstimate(
            flops=10 * groups * n * frames * rows * cols * head_dim,
            bytes_accessed=2 * 2 * groups * n * frames * rows * cols * head_dim,
            transcendentals=0,
        ),
        name="pack",
    )(*([qkv] * len(parts)), q_gain.reshape(1, -1), k_gain.reshape(1, -1))


def attend_kernel(
    head, q_slot, span, reach, scale,
    info_ref, c_ref, t0_ref, t1_ref, h0_ref, h1_ref, q_ref, out_ref, k_ref, v_ref, bias_ref,
):
    groups, _, frames, own, head_dim = c_ref.shape
    rows = own // TW
    edge = TH * TW
    for slot, dst in ((0, k_ref), (1, v_ref)):
        dst[:, 0:TT, edge : edge + own] = t0_ref[:, slot]
        dst[:, TT : TT + frames, edge : edge + own] = c_ref[:, slot]
        dst[:, TT + frames : 2 * TT + frames, edge : edge + own] = t1_ref[:, slot]
        dst[:, :, 0:edge] = h0_ref[:, slot]
        dst[:, :, edge + own : 2 * edge + own] = h1_ref[:, slot]

    tiles_t = frames // TT
    tiles_h = rows // TH
    halves = groups // span
    nq = span * TT * edge
    nk = reach * 3 * TT * 3 * edge
    per_col = 3 * TT * 3 * edge
    rad_t = info_ref[3 * head]
    rad_h = info_ref[3 * head + 1]
    rad_w = info_ref[3 * head + 2]
    base_t = info_ref.shape[0] - (tiles_t + 2) - (tiles_h + 2)
    base_h = base_t + tiles_t + 2

    q_col = lax.broadcasted_iota(jnp.int32, (nq, nk), 0) // (TT * edge)
    k_col = lax.broadcasted_iota(jnp.int32, (nq, nk), 1) // per_col
    for half in range(halves):
        first = min(max(half * span - 1, 0), groups - reach)
        gap = jnp.abs(q_col + (half * span - first) - k_col)
        bias_ref[half] = jnp.where(gap <= rad_w, 0.0, NEG)

    at = lax.broadcasted_iota(jnp.int32, (1, nk), 1) % per_col
    k_frame = at // (3 * edge)
    k_row = (at % (3 * edge)) // TW
    at_q = lax.broadcasted_iota(jnp.int32, (nq, 1), 0) % (TT * edge)
    q_frame = at_q // edge
    q_row = (at_q % edge) // TW

    @pl.loop(0, tiles_t * tiles_h * halves)
    def _(step):
        half = step % halves
        th = (step // halves) % tiles_h
        tt = step // (halves * tiles_h)
        first = jnp.clip(half * span - 1, 0, groups - reach)
        ok_t = jnp.zeros((1, nk), jnp.bool_)
        ok_h = jnp.zeros((1, nk), jnp.bool_)
        for near in range(3):
            away = abs(near - 1)
            live_t = jnp.where(away <= rad_t, info_ref[base_t + tt + near], 0)
            live_h = jnp.where(away <= rad_h, info_ref[base_h + th + near], 0)
            ok_t = ok_t | ((k_frame // TT == near) & (k_frame % TT < live_t))
            ok_h = ok_h | ((k_row // TH == near) & (k_row % TH < live_h))
        key_bias = jnp.where(ok_t & ok_h, 0.0, NEG)
        q_rows = pl.ds(pl.multiple_of(th * edge, edge), edge)
        k_rows = pl.ds(pl.multiple_of(th * edge, edge), 3 * edge)
        q_cols = pl.ds(half * span, span)
        k_cols = pl.ds(first, reach)
        q_frames = pl.ds(tt * TT, TT)
        k_frames = pl.ds(tt * TT, 3 * TT)
        q = q_ref[q_cols, q_slot, q_frames, q_rows, :].reshape(nq, head_dim)
        k = k_ref[k_cols, k_frames, k_rows, :].reshape(nk, head_dim)
        v = v_ref[k_cols, k_frames, k_rows, :].reshape(nk, head_dim)
        scores = lax.dot_general(
            q, k, (((1,), (1,)), ((), ())), preferred_element_type=jnp.float32
        )
        scores = scores * scale + (bias_ref[half] + key_bias)
        top = jnp.max(scores, axis=1, keepdims=True)
        raised = jnp.exp(scores - top)
        summed = jnp.sum(raised, axis=1, keepdims=True)
        blended = jnp.dot(
            raised.astype(jnp.bfloat16), v, preferred_element_type=jnp.float32
        )
        live = (q_frame < info_ref[base_t + tt + 1]) & (q_row < info_ref[base_h + th + 1])
        result = jnp.where(live, blended / summed, 0.0).astype(jnp.bfloat16)
        out_ref[q_cols, q_frames, q_rows, :] = result.reshape(span, TT, edge, head_dim)


def attend(info, center, t0, t1, h0, h1, queries, head, q_slot):
    groups, _, frames, own, head_dim = center.shape
    span = groups // 2 if groups > 1 else groups
    reach = min(span + 1, groups)
    rows = own // TW
    edge = TH * TW
    nq = span * TT * edge
    nk = reach * 9 * TT * edge
    steps = (frames // TT) * (rows // TH) * (groups // span)
    vmem = pl.BlockSpec(memory_space=pltpu.VMEM)
    ext = (groups, frames + 2 * TT, own + 2 * edge, head_dim)
    return pl.pallas_call(
        functools.partial(attend_kernel, head, q_slot, span, reach, 1.0 / math.sqrt(head_dim)),
        in_specs=[pl.BlockSpec(memory_space=pltpu.SMEM)] + [vmem] * 6,
        out_specs=vmem,
        out_shape=jax.ShapeDtypeStruct((groups, frames, own, head_dim), jnp.bfloat16),
        scratch_shapes=[
            pltpu.VMEM(ext, jnp.bfloat16),
            pltpu.VMEM(ext, jnp.bfloat16),
            pltpu.VMEM((groups // span, nq, nk), jnp.float32),
        ],
        cost_estimate=pl.CostEstimate(
            flops=4 * steps * nq * nk * head_dim,
            bytes_accessed=4 << 20,
            transcendentals=steps * nq * nk,
        ),
        compiler_params=pltpu.CompilerParams(vmem_limit_bytes=40 << 20),
        name="attend",
    )(info, center, t0, t1, h0, h1, queries)


def unpack_kernel(*refs):
    out_ref = refs[-1]
    rows, cols = out_ref.shape[1:3]
    groups, _, own, head_dim = refs[0].shape
    heads = len(refs) - 1
    for head, ref in enumerate(refs[:-1]):
        for group in range(groups):
            at = (heads * group + head) * head_dim
            x = ref[group, 0].astype(jnp.float32).reshape(rows, cols, head_dim)
            out_ref[0, :, :, at : at + head_dim] = x.astype(jnp.bfloat16)


def unpack(pieces, rows, cols):
    groups, frames, own, head_dim = pieces[0].shape
    channels = groups * len(pieces) * head_dim
    return pl.pallas_call(
        unpack_kernel,
        grid=(frames,),
        in_specs=[pl.BlockSpec((groups, 1, own, head_dim), lambda f: (0, f, 0, 0))] * len(pieces),
        out_specs=pl.BlockSpec((1, rows, cols, channels), lambda f: (f, 0, 0, 0)),
        out_shape=jax.ShapeDtypeStruct((frames, rows, cols, channels), jnp.bfloat16),
        name="unpack",
    )(*pieces)


def shifted(value, axis, step):
    size = lax.axis_size(axis)
    if step > 0:
        return lax.ppermute(value, axis, [(i, i + 1) for i in range(size - 1)])
    return lax.ppermute(value, axis, [(i + 1, i) for i in range(size - 1)])


def exchange(value):
    return lax.all_to_all(value, "hd", split_axis=0, concat_axis=0, tiled=True)


def shards(qkv, q_gain, k_gain, windows, frame_counts, row_counts):
    frames, rows, cols, channels = qkv.shape
    head_dim = q_gain.shape[0]
    groups = lax.axis_size("hd")
    heads_local = channels // (3 * head_dim) // groups
    edge = TH * TW
    own = rows * cols
    tiles_t = frames // TT
    tiles_h = rows // TH
    near_t = lax.dynamic_slice(
        jnp.pad(frame_counts, (1, 1)), (lax.axis_index("ta") * tiles_t,), (tiles_t + 2,)
    )
    near_h = lax.dynamic_slice(
        jnp.pad(row_counts, (1, 1)), (lax.axis_index("ha") * tiles_h,), (tiles_h + 2,)
    )
    info = jnp.concatenate([windows.reshape(-1), near_t, near_h])

    plan = [[(1, head), (2, head)] for head in range(heads_local)]
    where_q = {}
    for head in range(heads_local):
        ride = min(head + 1, heads_local - 1)
        where_q[head] = (ride, len(plan[ride]))
        plan[ride].append((0, head))
    got = [exchange(pack(qkv, q_gain, k_gain, tuple(p), heads_local, groups)) for p in plan]

    outs = []
    for head in range(heads_local):
        center = got[head]
        pair = center[:, :2]
        t0 = shifted(pair[:, :, frames - TT :], "ta", 1)
        t1 = shifted(pair[:, :, :TT], "ta", -1)
        low = jnp.concatenate(
            [t0[:, :, :, :edge], pair[:, :, :, :edge], t1[:, :, :, :edge]], axis=2
        )
        high = jnp.concatenate(
            [t0[:, :, :, own - edge :], pair[:, :, :, own - edge :], t1[:, :, :, own - edge :]],
            axis=2,
        )
        h0 = shifted(high, "ha", 1)
        h1 = shifted(low, "ha", -1)
        ride, slot = where_q[head]
        out = attend(info, center, t0, t1, h0, h1, got[ride], head, slot)
        outs.append(exchange(out))
    return unpack(outs, rows, cols)


def solution(mesh):
    return jax.shard_map(
        shards,
        mesh=mesh,
        in_specs=(P("ta", "ha", "hd", None), P(), P(), P("hd", None), P(), P()),
        out_specs=P("ta", "ha", "hd", None),
        check_vma=False,
    )
```

```python
import functools
import math

import jax
import jax.numpy as jnp
from jax import lax
from jax.experimental import pallas as pl
from jax.experimental.pallas import tpu as pltpu
from jax.sharding import PartitionSpec as P


TT = 2
TH = 2
TW = 8
NEG = -1e30

GRANT = 62 << 20


def cost(flops, size, transcendentals=0):
    return pl.CostEstimate(flops=flops, bytes_accessed=size, transcendentals=transcendentals)


def pack_kernel(entries, parts, heads_local, tiles, *refs):
    part_refs = refs[: len(parts)]
    qg_ref, kg_ref, out_ref = refs[len(parts) : len(parts) + 3]
    rim_refs = refs[len(parts) + 3 :]
    frames, rows, cols = part_refs[0].shape[:3]
    groups = out_ref.shape[0]
    head_dim = qg_ref.shape[-1]
    gains = {0: qg_ref[...].reshape(1, 1, 1, head_dim), 1: kg_ref[...].reshape(1, 1, 1, head_dim)}
    for dest in range(groups):
        for slot, (part, head) in enumerate(entries):
            at = (heads_local * dest + head) * head_dim
            x = part_refs[parts.index(part)][:, :, :, at : at + head_dim].astype(jnp.float32)
            if part in gains:
                meansq = jnp.mean(x * x, axis=-1, keepdims=True)
                x = x * lax.rsqrt(meansq + 1e-06) * gains[part]
            x = x.reshape(frames, rows * cols, head_dim).astype(jnp.bfloat16)
            out_ref[dest, slot * frames : (slot + 1) * frames] = x
            if tiles:
                rim_refs[0][dest, slot * TT : (slot + 1) * TT] = x[:TT]
                rim_refs[1][dest, slot * TT : (slot + 1) * TT] = x[frames - TT :]


def whole(shape):
    return pl.BlockSpec(shape, lambda i: (0,) * len(shape))


def one_step(kernel, in_specs, outs, size):
    shapes = [jax.ShapeDtypeStruct(shape, jnp.bfloat16) for shape in outs]
    return pl.pallas_call(
        kernel,
        grid=(1,),
        in_specs=in_specs,
        out_specs=[whole(shape) for shape in outs],
        out_shape=shapes,
        cost_estimate=cost(size, size),
        compiler_params=pltpu.CompilerParams(vmem_limit_bytes=GRANT),
    )


def pack(qkv, q_gain, k_gain, entries, heads_local, groups, tiles=False):
    frames, rows, cols, channels = qkv.shape
    head_dim = q_gain.shape[-1]
    third = channels // 3
    parts = sorted({part for part, _ in entries})
    n = len(entries)
    own = rows * cols
    outs = [(groups, n * frames, own, head_dim)] + [(groups, n * TT, own, head_dim)] * (2 * tiles)
    in_specs = [
        pl.BlockSpec((frames, rows, cols, third), functools.partial(lambda p, i: (0, 0, 0, p), part))
        for part in parts
    ] + [whole((1, head_dim))] * 2
    kernel = functools.partial(pack_kernel, entries, parts, heads_local, tiles)
    packed = one_step(kernel, in_specs, outs, 4 * math.prod(outs[0]))(
        *([qkv] * len(parts)), q_gain.reshape(1, -1), k_gain.reshape(1, -1)
    )
    return packed if tiles else packed[0]


def join_kernel(frames, c_ref, t0_ref, t1_ref, q_ref, out_ref):
    long = frames + 2 * TT
    for kv in range(2):
        at = kv * long
        out_ref[:, at : at + TT] = t0_ref[:, kv * TT : (kv + 1) * TT]
        out_ref[:, at + TT : at + TT + frames] = c_ref[:, kv * frames : (kv + 1) * frames]
        out_ref[:, at + TT + frames : at + long] = t1_ref[:, kv * TT : (kv + 1) * TT]
    out_ref[:, 2 * long :] = q_ref[...]


def join(center, t0, t1, queries):
    groups, slabs, own, head_dim = center.shape
    frames = slabs // 2
    total = 2 * (frames + 2 * TT) + queries.shape[1]
    arrays = (center, t0, t1, queries)
    out = (groups, total, own, head_dim)
    return one_step(
        functools.partial(join_kernel, frames),
        [whole(a.shape) for a in arrays],
        [out],
        4 * math.prod(out),
    )(*arrays)[0]


def tiles_kernel(frames, ref, first_ref, last_ref):
    for n in range(ref.shape[1] // frames):
        to = slice(n * TT, (n + 1) * TT)
        first_ref[:, to] = ref[:, n * frames : n * frames + TT]
        last_ref[:, to] = ref[:, (n + 1) * frames - TT : (n + 1) * frames]


def tiles_of(value, frames):
    groups, slabs, own, head_dim = value.shape
    out = (groups, slabs // frames * TT, own, head_dim)
    return one_step(
        functools.partial(tiles_kernel, frames),
        [whole(value.shape)],
        [out, out],
        8 * math.prod(out),
    )(value)


def rim_kernel(edge, counts, *refs):
    low_ref, high_ref = refs[-2:]
    sources = refs[:-2]
    own = sources[0].shape[2]
    total = sum(counts)
    for n in range(low_ref.shape[1] // total):
        at = n * total
        for ref, count in zip(sources, counts):
            src = slice(n * count, (n + 1) * count)
            low_ref[:, at : at + count] = ref[:, src, 0:edge]
            high_ref[:, at : at + count] = ref[:, src, own - edge : own]
            at += count


def rim(arrays, counts, heads, edge):
    groups, _, own, head_dim = arrays[0].shape
    out = (groups, heads * sum(counts), edge, head_dim)
    in_specs = [whole((groups, heads * c, own, head_dim)) for c in counts]
    return one_step(
        functools.partial(rim_kernel, edge, counts), in_specs, [out, out], 8 * math.prod(out)
    )(*arrays)


def attend_kernel(pieces, frames, span, reach, scale, slot, info_ref, *refs):
    count = len(pieces)
    piece_refs = refs[:count]
    q_ref = refs[count]
    out_ref, k_ref, v_ref, bias_ref = refs[-4:]
    here = slot + pl.program_id(0)
    if len(refs) > count + 5:
        out_ref[:, 0:slot] = refs[count + 1][...]
    groups = q_ref.shape[0]
    own, head_dim = q_ref.shape[2:]
    edge = TH * TW
    for ref, (spans, low) in zip(piece_refs, pieces):
        tokens = slice(low, low + ref.shape[2])
        at = 0
        for dst in (k_ref, v_ref):
            for start, n in spans:
                dst[:, start : start + n, tokens] = ref[:, at : at + n]
                at += n

    tiles_t = frames // TT
    tiles_h = own // edge
    halves = groups // span
    per_col = 3 * TT * 3 * edge
    nq = span * TT * edge
    nk = reach * per_col
    firsts = [min(max(half * span - 1, 0), groups - reach) for half in range(halves)]
    base_t = info_ref.shape[0] - (tiles_t + 2) - (tiles_h + 2)
    base_h = base_t + tiles_t + 2
    head = here
    rad_t = info_ref[3 * head]
    rad_h = info_ref[3 * head + 1]
    rad_w = info_ref[3 * head + 2]

    q_col = lax.broadcasted_iota(jnp.int32, (nq, nk), 0) // (TT * edge)
    k_col = lax.broadcasted_iota(jnp.int32, (nq, nk), 1) // per_col
    for half, first in enumerate(firsts):
        gap = jnp.abs(q_col - k_col + (half * span - first))
        bias_ref[half] = jnp.where(gap <= rad_w, 0.0, NEG)

    at = lax.broadcasted_iota(jnp.int32, (1, nk), 1) % per_col
    k_frame = at // (3 * edge)
    k_row = (at % (3 * edge)) // TW
    at_q = lax.broadcasted_iota(jnp.int32, (nq, 1), 0) % (TT * edge)
    q_frame = at_q // edge
    q_row = (at_q % edge) // TW

    @pl.loop(0, tiles_t * tiles_h)
    def _(step):
        th = step % tiles_h
        tt = step // tiles_h
        ok_t = jnp.zeros((1, nk), jnp.bool_)
        ok_h = jnp.zeros((1, nk), jnp.bool_)
        for near in range(3):
            away = abs(near - 1)
            live_t = jnp.where(away <= rad_t, info_ref[base_t + tt + near], 0)
            live_h = jnp.where(away <= rad_h, info_ref[base_h + th + near], 0)
            ok_t = ok_t | ((k_frame // TT == near) & (k_frame % TT < live_t))
            ok_h = ok_h | ((k_row // TH == near) & (k_row % TH < live_h))
        key_bias = jnp.where(ok_t & ok_h, 0.0, NEG)
        live = (q_frame < info_ref[base_t + tt + 1]) & (q_row < info_ref[base_h + th + 1])
        q_rows = pl.ds(pl.multiple_of(th * edge, edge), edge)
        k_rows = pl.ds(pl.multiple_of(th * edge, edge), 3 * edge)
        q_frames = pl.ds(tt * TT, TT)
        k_frames = pl.ds(tt * TT, 3 * TT)
        for half, first in enumerate(firsts):
            q_cols = slice(half * span, (half + 1) * span)
            k_cols = slice(first, first + reach)
            q = q_ref[q_cols, q_frames, q_rows, :].reshape(nq, head_dim)
            k = k_ref[k_cols, k_frames, k_rows, :].reshape(nk, head_dim)
            v = v_ref[k_cols, k_frames, k_rows, :].reshape(nk, head_dim)
            scores = lax.dot_general(
                q, k, (((1,), (1,)), ((), ())), preferred_element_type=jnp.float32
            )
            scores = scores * scale + (bias_ref[half] + key_bias)
            top = jnp.max(scores, axis=1, keepdims=True)
            raised = jnp.exp2(scores - top)
            summed = jnp.sum(raised, axis=1, keepdims=True)
            blended = jnp.dot(
                raised.astype(jnp.bfloat16), v, preferred_element_type=jnp.float32
            )
            result = jnp.where(live, blended / summed, 0.0).astype(jnp.bfloat16)
            out_ref[q_cols, here, q_frames, q_rows, :] = result.reshape(span, TT, edge, head_dim)


def attend(info, pieces, queries, q_block, heads, slot, before, frames):
    groups, _, own, head_dim = queries.shape
    span = max(groups // 2, 1)
    reach = min(span + 1, groups)
    edge = TH * TW
    nq = span * TT * edge
    nk = reach * 9 * TT * edge
    steps = heads * (frames // TT) * (own // edge) * (groups // span)
    ext = (groups, frames + 2 * TT, own + 2 * edge, head_dim)
    in_specs = [pl.BlockSpec(memory_space=pltpu.SMEM)]
    in_specs += [
        pl.BlockSpec(
            (groups, 2 * sum(n for _, n in spans), a.shape[2], head_dim), lambda h: (0, h, 0, 0)
        )
        for a, spans, _ in pieces
    ]
    in_specs += [
        pl.BlockSpec((groups, frames, own, head_dim), lambda h: (0, q_block + slot + h, 0, 0)),
    ]
    args = [info, *(a for a, _, _ in pieces), queries]
    total = slot + heads
    if before is not None:
        in_specs.append(pl.BlockSpec(before.shape, lambda h: (0, 0, 0, 0, 0)))
        args.append(before)
    return pl.pallas_call(
        functools.partial(
            attend_kernel,
            tuple((spans, low) for _, spans, low in pieces),
            frames,
            span,
            reach,
            math.log2(math.e) / math.sqrt(head_dim),
            slot,
        ),
        grid=(heads,),
        in_specs=in_specs,
        out_specs=pl.BlockSpec(memory_space=pltpu.VMEM),
        out_shape=pltpu.VMEM((groups, total, frames, own, head_dim), jnp.bfloat16),
        scratch_shapes=[
            pltpu.VMEM(ext, jnp.bfloat16),
            pltpu.VMEM(ext, jnp.bfloat16),
            pltpu.VMEM((groups // span, nq, nk), jnp.float32),
        ],
        cost_estimate=cost(4 * steps * nq * nk * head_dim, heads * (4 << 20), steps * nq * nk),
        compiler_params=pltpu.CompilerParams(vmem_limit_bytes=GRANT),
        name="attend",
    )(*args)


def unpack_kernel(in_ref, out_ref):
    frames, rows, cols = out_ref.shape[:3]
    groups, heads, _, _, head_dim = in_ref.shape
    for head in range(heads):
        for group in range(groups):
            at = (heads * group + head) * head_dim
            x = in_ref[group, head].astype(jnp.float32).reshape(frames, rows, cols, head_dim)
            out_ref[:, :, :, at : at + head_dim] = x.astype(jnp.bfloat16)


def unpack(value, rows, cols):
    groups, heads, frames, _, head_dim = value.shape
    out = (frames, rows, cols, groups * heads * head_dim)
    return pl.pallas_call(
        unpack_kernel,
        in_specs=[pl.BlockSpec(memory_space=pltpu.VMEM)],
        out_specs=pl.BlockSpec(memory_space=pltpu.VMEM),
        out_shape=jax.ShapeDtypeStruct(out, jnp.bfloat16),
        compiler_params=pltpu.CompilerParams(vmem_limit_bytes=16 << 20),
        name="unpack",
    )(value)


def shifted(value, axis, step):
    size = lax.axis_size(axis)
    pairs = [(i, i + 1) if step > 0 else (i + 1, i) for i in range(size - 1)]
    return lax.ppermute(value, axis, pairs)


def exchange(value):
    return lax.all_to_all(value, "hd", split_axis=0, concat_axis=0, tiled=True)


def shards(qkv, q_gain, k_gain, windows, frame_counts, row_counts):
    frames, rows, cols, channels = qkv.shape
    head_dim = q_gain.shape[0]
    groups = lax.axis_size("hd")
    heads = channels // (3 * head_dim) // groups
    edge = TH * TW
    own = rows * cols
    tiles_t = frames // TT
    tiles_h = rows // TH
    near_t = lax.dynamic_slice(
        jnp.pad(frame_counts, (1, 1)), (lax.axis_index("ta") * tiles_t,), (tiles_t + 2,)
    )
    near_h = lax.dynamic_slice(
        jnp.pad(row_counts, (1, 1)), (lax.axis_index("ha") * tiles_h,), (tiles_h + 2,)
    )
    info = jnp.concatenate([windows.reshape(-1), near_t, near_h])

    def packed(entries, tiles=False):
        return pack(qkv, q_gain, k_gain, tuple(entries), heads, groups, tiles)

    rest = heads - 1
    long = frames + 2 * TT
    value_z, first_z, last_z = packed([(1, rest), (2, rest)], True)
    tz0 = shifted(last_z, "ta", 1)
    tz1 = shifted(first_z, "ta", -1)
    value_n = packed([(part, head) for head in range(rest) for part in (1, 2)])
    got_n = exchange(value_n)
    value_q = packed([(0, head) for head in range(heads)])
    joined = join(value_z, tz0, tz1, value_q)
    got_z = exchange(joined)

    first_n, last_n = tiles_of(got_n, frames)
    tn0 = shifted(last_n, "ta", 1)
    tn1 = shifted(first_n, "ta", -1)
    low_c, high_c = rim((got_n,), (frames,), 2 * rest, edge)
    hc0 = shifted(high_c, "ha", 1)
    hc1 = shifted(low_c, "ha", -1)
    low_z, high_z = rim((got_z,), (long,), 2, edge)
    hz0 = shifted(high_z, "ha", 1)
    hz1 = shifted(low_z, "ha", -1)
    low_t, high_t = rim((tn0, tn1), (TT, TT), 2 * rest, edge)
    ht0 = shifted(high_t, "ha", 1)
    ht1 = shifted(low_t, "ha", -1)

    q_block = 2 * long // frames
    mine, every = ((TT, frames),), ((0, long),)
    beside = ((0, TT), (TT + frames, TT))
    pieces_n = (
        (got_n, mine, edge),
        (tn0, ((0, TT),), edge),
        (tn1, ((TT + frames, TT),), edge),
        (hc0, mine, 0),
        (hc1, mine, edge + own),
        (ht0, beside, 0),
        (ht1, beside, edge + own),
    )
    pieces_z = ((got_z, every, edge), (hz0, every, 0), (hz1, every, edge + own))
    out = attend(info, pieces_n, got_z, q_block, rest, 0, None, frames)
    out = attend(info, pieces_z, got_z, q_block, 1, rest, out, frames)
    return unpack(exchange(out), rows, cols)


def solution(mesh):
    return jax.shard_map(
        shards,
        mesh=mesh,
        in_specs=(P("ta", "ha", "hd", None), P(), P(), P("hd", None), P(), P()),
        out_specs=P("ta", "ha", "hd", None),
        check_vma=False,
    )
```

```python
import functools
import math

import jax
import jax.numpy as jnp
from jax import lax
from jax.experimental import pallas as pl
from jax.experimental.pallas import tpu as pltpu
from jax.sharding import PartitionSpec as P


TT = 2
TH = 2
TW = 8
NEG = -1e30

GRANT = 24 << 20
PACK_GRANT = 62 << 20


def cost(flops, size, transcendentals=0):
    return pl.CostEstimate(flops=flops, bytes_accessed=size, transcendentals=transcendentals)


def pack_kernel(entries, parts, heads_local, tiles, *refs):
    part_refs = refs[: len(parts)]
    qg_ref, kg_ref, out_ref = refs[len(parts) : len(parts) + 3]
    rim_refs = refs[len(parts) + 3 :]
    frames, rows, cols = part_refs[0].shape[:3]
    groups = out_ref.shape[0]
    head_dim = qg_ref.shape[-1]
    gains = {0: qg_ref[...].reshape(1, 1, 1, head_dim), 1: kg_ref[...].reshape(1, 1, 1, head_dim)}
    for dest in range(groups):
        for slot, (part, head) in enumerate(entries):
            at = (heads_local * dest + head) * head_dim
            x = part_refs[parts.index(part)][:, :, :, at : at + head_dim].astype(jnp.float32)
            if part in gains:
                meansq = jnp.mean(x * x, axis=-1, keepdims=True)
                x = x * lax.rsqrt(meansq + 1e-06) * gains[part]
            x = x.reshape(frames, rows * cols, head_dim).astype(jnp.bfloat16)
            out_ref[dest, slot * frames : (slot + 1) * frames] = x
            if tiles:
                rim_refs[0][dest, slot * TT : (slot + 1) * TT] = x[:TT]
                rim_refs[1][dest, slot * TT : (slot + 1) * TT] = x[frames - TT :]


def whole(shape):
    return pl.BlockSpec(shape, lambda i: (0,) * len(shape))


def one_step(kernel, in_specs, outs, size, grant=None):
    shapes = [jax.ShapeDtypeStruct(shape, jnp.bfloat16) for shape in outs]
    return pl.pallas_call(
        kernel,
        grid=(1,),
        in_specs=in_specs,
        out_specs=[whole(shape) for shape in outs],
        out_shape=shapes,
        cost_estimate=cost(size, size),
        compiler_params=pltpu.CompilerParams(vmem_limit_bytes=grant or GRANT),
    )


def pack(qkv, q_gain, k_gain, entries, heads_local, groups, tiles=False):
    frames, rows, cols, channels = qkv.shape
    head_dim = q_gain.shape[-1]
    third = channels // 3
    parts = sorted({part for part, _ in entries})
    n = len(entries)
    own = rows * cols
    outs = [(groups, n * frames, own, head_dim)] + [(groups, n * TT, own, head_dim)] * (2 * tiles)
    in_specs = [
        pl.BlockSpec((frames, rows, cols, third), functools.partial(lambda p, i: (0, 0, 0, p), part))
        for part in parts
    ] + [whole((1, head_dim))] * 2
    kernel = functools.partial(pack_kernel, entries, parts, heads_local, tiles)
    packed = one_step(kernel, in_specs, outs, 4 * math.prod(outs[0]), PACK_GRANT)(
        *([qkv] * len(parts)), q_gain.reshape(1, -1), k_gain.reshape(1, -1)
    )
    return packed if tiles else packed[0]


def join_kernel(frames, c_ref, t0_ref, t1_ref, out_ref):
    long = frames + 2 * TT
    for kv in range(2):
        at = kv * long
        out_ref[:, at : at + TT] = t0_ref[:, kv * TT : (kv + 1) * TT]
        out_ref[:, at + TT : at + TT + frames] = c_ref[:, kv * frames : (kv + 1) * frames]
        out_ref[:, at + TT + frames : at + long] = t1_ref[:, kv * TT : (kv + 1) * TT]


def join(center, t0, t1):
    groups, slabs, own, head_dim = center.shape
    frames = slabs // 2
    total = 2 * (frames + 2 * TT)
    arrays = (center, t0, t1)
    out = (groups, total, own, head_dim)
    return one_step(
        functools.partial(join_kernel, frames),
        [whole(a.shape) for a in arrays],
        [out],
        4 * math.prod(out),
        PACK_GRANT,
    )(*arrays)[0]


def tiles_kernel(frames, ref, first_ref, last_ref):
    for n in range(ref.shape[1] // frames):
        to = slice(n * TT, (n + 1) * TT)
        first_ref[:, to] = ref[:, n * frames : n * frames + TT]
        last_ref[:, to] = ref[:, (n + 1) * frames - TT : (n + 1) * frames]


def tiles_of(value, frames):
    groups, slabs, own, head_dim = value.shape
    out = (groups, slabs // frames * TT, own, head_dim)
    return one_step(
        functools.partial(tiles_kernel, frames),
        [whole(value.shape)],
        [out, out],
        8 * math.prod(out),
    )(value)


def rim_kernel(edge, counts, *refs):
    low_ref, high_ref = refs[-2:]
    sources = refs[:-2]
    own = sources[0].shape[2]
    total = sum(counts)
    for n in range(low_ref.shape[1] // total):
        at = n * total
        for ref, count in zip(sources, counts):
            src = slice(n * count, (n + 1) * count)
            low_ref[:, at : at + count] = ref[:, src, 0:edge]
            high_ref[:, at : at + count] = ref[:, src, own - edge : own]
            at += count


def rim(arrays, counts, heads, edge):
    groups, _, own, head_dim = arrays[0].shape
    out = (groups, heads * sum(counts), edge, head_dim)
    in_specs = [whole((groups, heads * c, own, head_dim)) for c in counts]
    return one_step(
        functools.partial(rim_kernel, edge, counts), in_specs, [out, out], 8 * math.prod(out)
    )(*arrays)


def attend_kernel(pieces, frames, span, reach, scale, slot, info_ref, *refs):
    count = len(pieces)
    piece_refs = refs[:count]
    q_ref = refs[count]
    out_ref, k_ref, v_ref, bias_ref = refs[-4:]
    here = slot + pl.program_id(0)
    if len(refs) > count + 5:
        out_ref[:, 0:slot] = refs[count + 1][...]
    groups = q_ref.shape[0]
    own, head_dim = q_ref.shape[2:]
    edge = TH * TW
    for ref, (spans, low) in zip(piece_refs, pieces):
        tokens = slice(low, low + ref.shape[2])
        at = 0
        for dst in (k_ref, v_ref):
            for start, n in spans:
                dst[:, start : start + n, tokens] = ref[:, at : at + n]
                at += n

    tiles_t = frames // TT
    tiles_h = own // edge
    halves = groups // span
    per_col = 3 * TT * 3 * edge
    nq = span * TT * edge
    nk = reach * per_col
    firsts = [min(max(half * span - 1, 0), groups - reach) for half in range(halves)]
    base_t = info_ref.shape[0] - (tiles_t + 2) - (tiles_h + 2)
    base_h = base_t + tiles_t + 2
    head = here
    rad_t = info_ref[3 * head]
    rad_h = info_ref[3 * head + 1]
    rad_w = info_ref[3 * head + 2]

    q_col = lax.broadcasted_iota(jnp.int32, (nq, nk), 0) // (TT * edge)
    k_col = lax.broadcasted_iota(jnp.int32, (nq, nk), 1) // per_col
    for half, first in enumerate(firsts):
        gap = jnp.abs(q_col - k_col + (half * span - first))
        bias_ref[half] = jnp.where(gap <= rad_w, 0.0, NEG)

    at = lax.broadcasted_iota(jnp.int32, (1, nk), 1) % per_col
    k_frame = at // (3 * edge)
    k_row = (at % (3 * edge)) // TW
    at_q = lax.broadcasted_iota(jnp.int32, (nq, 1), 0) % (TT * edge)
    q_frame = at_q // edge
    q_row = (at_q % edge) // TW

    @pl.loop(0, tiles_t * tiles_h)
    def _(step):
        th = step % tiles_h
        tt = step // tiles_h
        ok_t = jnp.zeros((1, nk), jnp.bool_)
        ok_h = jnp.zeros((1, nk), jnp.bool_)
        for near in range(3):
            away = abs(near - 1)
            live_t = jnp.where(away <= rad_t, info_ref[base_t + tt + near], 0)
            live_h = jnp.where(away <= rad_h, info_ref[base_h + th + near], 0)
            ok_t = ok_t | ((k_frame // TT == near) & (k_frame % TT < live_t))
            ok_h = ok_h | ((k_row // TH == near) & (k_row % TH < live_h))
        key_bias = jnp.where(ok_t & ok_h, 0.0, NEG)
        live = (q_frame < info_ref[base_t + tt + 1]) & (q_row < info_ref[base_h + th + 1])
        q_rows = pl.ds(pl.multiple_of(th * edge, edge), edge)
        k_rows = pl.ds(pl.multiple_of(th * edge, edge), 3 * edge)
        q_frames = pl.ds(tt * TT, TT)
        k_frames = pl.ds(tt * TT, 3 * TT)
        for half, first in enumerate(firsts):
            q_cols = slice(half * span, (half + 1) * span)
            k_cols = slice(first, first + reach)
            q = q_ref[q_cols, q_frames, q_rows, :].reshape(nq, head_dim)
            k = k_ref[k_cols, k_frames, k_rows, :].reshape(nk, head_dim)
            v = v_ref[k_cols, k_frames, k_rows, :].reshape(nk, head_dim)
            scores = lax.dot_general(
                q, k, (((1,), (1,)), ((), ())), preferred_element_type=jnp.float32
            )
            scores = scores * scale + (bias_ref[half] + key_bias)
            top = jnp.max(scores, axis=1, keepdims=True)
            raised = jnp.exp2(scores - top)
            summed = jnp.sum(raised, axis=1, keepdims=True)
            blended = jnp.dot(
                raised.astype(jnp.bfloat16), v, preferred_element_type=jnp.float32
            )
            result = jnp.where(live, blended / summed, 0.0).astype(jnp.bfloat16)
            out_ref[q_cols, here, q_frames, q_rows, :] = result.reshape(span, TT, edge, head_dim)


def attend(info, pieces, queries, heads, slot, before, frames):
    groups, _, own, head_dim = queries.shape
    span = max(groups // 2, 1)
    reach = min(span + 1, groups)
    edge = TH * TW
    nq = span * TT * edge
    nk = reach * 9 * TT * edge
    steps = heads * (frames // TT) * (own // edge) * (groups // span)
    ext = (groups, frames + 2 * TT, own + 2 * edge, head_dim)
    in_specs = [pl.BlockSpec(memory_space=pltpu.SMEM)]
    in_specs += [
        pl.BlockSpec(
            (groups, 2 * sum(n for _, n in spans), a.shape[2], head_dim), lambda h: (0, h, 0, 0)
        )
        for a, spans, _ in pieces
    ]
    in_specs += [
        pl.BlockSpec((groups, frames, own, head_dim), lambda h: (0, slot + h, 0, 0)),
    ]
    args = [info, *(a for a, _, _ in pieces), queries]
    total = slot + heads
    if before is not None:
        in_specs.append(pl.BlockSpec(before.shape, lambda h: (0, 0, 0, 0, 0)))
        args.append(before)
    return pl.pallas_call(
        functools.partial(
            attend_kernel,
            tuple((spans, low) for _, spans, low in pieces),
            frames,
            span,
            reach,
            math.log2(math.e) / math.sqrt(head_dim),
            slot,
        ),
        grid=(heads,),
        in_specs=in_specs,
        out_specs=pl.BlockSpec(memory_space=pltpu.VMEM),
        out_shape=pltpu.VMEM((groups, total, frames, own, head_dim), jnp.bfloat16),
        scratch_shapes=[
            pltpu.VMEM(ext, jnp.bfloat16),
            pltpu.VMEM(ext, jnp.bfloat16),
            pltpu.VMEM((groups // span, nq, nk), jnp.float32),
        ],
        cost_estimate=cost(4 * steps * nq * nk * head_dim, heads * (4 << 20), steps * nq * nk),
        compiler_params=pltpu.CompilerParams(vmem_limit_bytes=GRANT),
        name="attend",
    )(*args)


def unpack_kernel(in_ref, out_ref):
    frames, rows, cols = out_ref.shape[:3]
    groups, heads, _, _, head_dim = in_ref.shape
    for head in range(heads):
        for group in range(groups):
            at = (heads * group + head) * head_dim
            x = in_ref[group, head].astype(jnp.float32).reshape(frames, rows, cols, head_dim)
            out_ref[:, :, :, at : at + head_dim] = x.astype(jnp.bfloat16)


def unpack(value, rows, cols):
    groups, heads, frames, _, head_dim = value.shape
    out = (frames, rows, cols, groups * heads * head_dim)
    return pl.pallas_call(
        unpack_kernel,
        in_specs=[pl.BlockSpec(memory_space=pltpu.VMEM)],
        out_specs=pl.BlockSpec(memory_space=pltpu.VMEM),
        out_shape=jax.ShapeDtypeStruct(out, jnp.bfloat16),
        compiler_params=pltpu.CompilerParams(vmem_limit_bytes=16 << 20),
        name="unpack",
    )(value)


def shifted(value, axis, step):
    size = lax.axis_size(axis)
    pairs = [(i, i + 1) if step > 0 else (i + 1, i) for i in range(size - 1)]
    return lax.ppermute(value, axis, pairs)


def exchange(value):
    return lax.all_to_all(value, "hd", split_axis=0, concat_axis=0, tiled=True)


def shards(qkv, q_gain, k_gain, windows, frame_counts, row_counts):
    frames, rows, cols, channels = qkv.shape
    head_dim = q_gain.shape[0]
    groups = lax.axis_size("hd")
    heads = channels // (3 * head_dim) // groups
    edge = TH * TW
    own = rows * cols
    tiles_t = frames // TT
    tiles_h = rows // TH
    near_t = lax.dynamic_slice(
        jnp.pad(frame_counts, (1, 1)), (lax.axis_index("ta") * tiles_t,), (tiles_t + 2,)
    )
    near_h = lax.dynamic_slice(
        jnp.pad(row_counts, (1, 1)), (lax.axis_index("ha") * tiles_h,), (tiles_h + 2,)
    )
    info = jnp.concatenate([windows.reshape(-1), near_t, near_h])

    def packed(entries, tiles=False):
        return pack(qkv, q_gain, k_gain, tuple(entries), heads, groups, tiles)

    rest = heads - 1
    long = frames + 2 * TT
    value_z, first_z, last_z = packed([(1, rest), (2, rest)], True)
    tz0 = shifted(last_z, "ta", 1)
    tz1 = shifted(first_z, "ta", -1)
    value_n = packed([(part, head) for head in range(rest) for part in (1, 2)])
    got_n = exchange(value_n)
    got_q = exchange(packed([(0, head) for head in range(heads)]))
    joined = join(value_z, tz0, tz1)
    got_z = exchange(joined)

    first_n, last_n = tiles_of(got_n, frames)
    tn0 = shifted(last_n, "ta", 1)
    tn1 = shifted(first_n, "ta", -1)
    low_c, high_c = rim((got_n,), (frames,), 2 * rest, edge)
    hc0 = shifted(high_c, "ha", 1)
    hc1 = shifted(low_c, "ha", -1)
    low_z, high_z = rim((got_z,), (long,), 2, edge)
    hz0 = shifted(high_z, "ha", 1)
    hz1 = shifted(low_z, "ha", -1)
    low_t, high_t = rim((tn0, tn1), (TT, TT), 2 * rest, edge)
    ht0 = shifted(high_t, "ha", 1)
    ht1 = shifted(low_t, "ha", -1)

    mine, every = ((TT, frames),), ((0, long),)
    beside = ((0, TT), (TT + frames, TT))
    pieces_n = (
        (got_n, mine, edge),
        (tn0, ((0, TT),), edge),
        (tn1, ((TT + frames, TT),), edge),
        (hc0, mine, 0),
        (hc1, mine, edge + own),
        (ht0, beside, 0),
        (ht1, beside, edge + own),
    )
    pieces_z = ((got_z, every, edge), (hz0, every, 0), (hz1, every, edge + own))
    out = attend(info, pieces_n, got_q, rest, 0, None, frames)
    out = attend(info, pieces_z, got_q, 1, rest, out, frames)
    return unpack(exchange(out), rows, cols)


def solution(mesh):
    return jax.shard_map(
        shards,
        mesh=mesh,
        in_specs=(P("ta", "ha", "hd", None), P(), P(), P("hd", None), P(), P()),
        out_specs=P("ta", "ha", "hd", None),
        check_vma=False,
    )
```

```python
import functools
import math

import jax
import jax.numpy as jnp
from jax import lax
from jax.experimental import pallas as pl
from jax.experimental.pallas import tpu as pltpu
from jax.sharding import PartitionSpec as P


TT = 2
TH = 2
TW = 8
NEG = -1e30

GRANT = 24 << 20
PACK_GRANT = 62 << 20


def cost(flops, size, transcendentals=0):
    return pl.CostEstimate(flops=flops, bytes_accessed=size, transcendentals=transcendentals)


def pack_kernel(entries, parts, heads_local, tiles, *refs):
    part_refs = refs[: len(parts)]
    qg_ref, kg_ref, out_ref = refs[len(parts) : len(parts) + 3]
    rim_refs = refs[len(parts) + 3 :]
    frames, rows, cols = part_refs[0].shape[:3]
    groups = out_ref.shape[0]
    head_dim = qg_ref.shape[-1]
    gains = {0: qg_ref[...].reshape(1, 1, 1, head_dim), 1: kg_ref[...].reshape(1, 1, 1, head_dim)}
    for dest in range(groups):
        for slot, (part, head) in enumerate(entries):
            at = (heads_local * dest + head) * head_dim
            x = part_refs[parts.index(part)][:, :, :, at : at + head_dim].astype(jnp.float32)
            if part in gains:
                meansq = jnp.mean(x * x, axis=-1, keepdims=True)
                x = x * lax.rsqrt(meansq + 1e-06) * gains[part]
            x = x.reshape(frames, rows * cols, head_dim).astype(jnp.bfloat16)
            out_ref[dest, slot * frames : (slot + 1) * frames] = x
            if tiles:
                rim_refs[0][dest, slot * TT : (slot + 1) * TT] = x[:TT]
                rim_refs[1][dest, slot * TT : (slot + 1) * TT] = x[frames - TT :]


def whole(shape):
    return pl.BlockSpec(shape, lambda i: (0,) * len(shape))


def one_step(kernel, in_specs, outs, size, grant=None):
    shapes = [jax.ShapeDtypeStruct(shape, jnp.bfloat16) for shape in outs]
    return pl.pallas_call(
        kernel,
        grid=(1,),
        in_specs=in_specs,
        out_specs=[whole(shape) for shape in outs],
        out_shape=shapes,
        cost_estimate=cost(size, size),
        compiler_params=pltpu.CompilerParams(vmem_limit_bytes=grant or GRANT),
    )


def pack(qkv, q_gain, k_gain, entries, heads_local, groups, tiles=False):
    frames, rows, cols, channels = qkv.shape
    head_dim = q_gain.shape[-1]
    third = channels // 3
    parts = sorted({part for part, _ in entries})
    n = len(entries)
    own = rows * cols
    outs = [(groups, n * frames, own, head_dim)] + [(groups, n * TT, own, head_dim)] * (2 * tiles)
    in_specs = [
        pl.BlockSpec((frames, rows, cols, third), functools.partial(lambda p, i: (0, 0, 0, p), part))
        for part in parts
    ] + [whole((1, head_dim))] * 2
    kernel = functools.partial(pack_kernel, entries, parts, heads_local, tiles)
    packed = one_step(kernel, in_specs, outs, 4 * math.prod(outs[0]), PACK_GRANT)(
        *([qkv] * len(parts)), q_gain.reshape(1, -1), k_gain.reshape(1, -1)
    )
    return packed if tiles else packed[0]


def join_kernel(frames, c_ref, t0_ref, t1_ref, out_ref):
    long = frames + 2 * TT
    for kv in range(2):
        at = kv * long
        out_ref[:, at : at + TT] = t0_ref[:, kv * TT : (kv + 1) * TT]
        out_ref[:, at + TT : at + TT + frames] = c_ref[:, kv * frames : (kv + 1) * frames]
        out_ref[:, at + TT + frames : at + long] = t1_ref[:, kv * TT : (kv + 1) * TT]


def join(center, t0, t1):
    groups, slabs, own, head_dim = center.shape
    frames = slabs // 2
    total = 2 * (frames + 2 * TT)
    arrays = (center, t0, t1)
    out = (groups, total, own, head_dim)
    return one_step(
        functools.partial(join_kernel, frames),
        [whole(a.shape) for a in arrays],
        [out],
        4 * math.prod(out),
        PACK_GRANT,
    )(*arrays)[0]


def tiles_kernel(frames, ref, first_ref, last_ref):
    for n in range(ref.shape[1] // frames):
        to = slice(n * TT, (n + 1) * TT)
        first_ref[:, to] = ref[:, n * frames : n * frames + TT]
        last_ref[:, to] = ref[:, (n + 1) * frames - TT : (n + 1) * frames]


def tiles_of(value, frames):
    groups, slabs, own, head_dim = value.shape
    out = (groups, slabs // frames * TT, own, head_dim)
    return one_step(
        functools.partial(tiles_kernel, frames),
        [whole(value.shape)],
        [out, out],
        8 * math.prod(out),
    )(value)


def rim_kernel(edge, counts, *refs):
    low_ref, high_ref = refs[-2:]
    sources = refs[:-2]
    own = sources[0].shape[2]
    total = sum(counts)
    for n in range(low_ref.shape[1] // total):
        at = n * total
        for ref, count in zip(sources, counts):
            src = slice(n * count, (n + 1) * count)
            low_ref[:, at : at + count] = ref[:, src, 0:edge]
            high_ref[:, at : at + count] = ref[:, src, own - edge : own]
            at += count


def rim(arrays, counts, heads, edge):
    groups, _, own, head_dim = arrays[0].shape
    out = (groups, heads * sum(counts), edge, head_dim)
    in_specs = [whole((groups, heads * c, own, head_dim)) for c in counts]
    return one_step(
        functools.partial(rim_kernel, edge, counts), in_specs, [out, out], 8 * math.prod(out)
    )(*arrays)


def attend_kernel(pieces, frames, span, reach, scale, head, slot, info_ref, *refs):
    count = len(pieces)
    piece_refs = refs[:count]
    q_ref = refs[count]
    out_ref, k_ref, v_ref, bias_ref = refs[-4:]
    here = slot + pl.program_id(0)
    if len(refs) > count + 5:
        out_ref[:, 0:slot] = refs[count + 1][...]
    groups = q_ref.shape[0]
    own, head_dim = q_ref.shape[2:]
    edge = TH * TW
    for ref, (spans, low) in zip(piece_refs, pieces):
        tokens = slice(low, low + ref.shape[2])
        at = 0
        for dst in (k_ref, v_ref):
            for start, n in spans:
                dst[:, start : start + n, tokens] = ref[:, at : at + n]
                at += n

    tiles_t = frames // TT
    tiles_h = own // edge
    base_t = info_ref.shape[0] - (tiles_t + 2) - (tiles_h + 2)
    base_h = base_t + tiles_t + 2
    head = head + pl.program_id(0)
    rad_t = info_ref[3 * head]
    rad_h = info_ref[3 * head + 1]
    rad_w = info_ref[3 * head + 2]
    nq = span * TT * edge
    at_q = lax.broadcasted_iota(jnp.int32, (nq, 1), 0) % (TT * edge)
    q_frame = at_q // edge
    q_row = (at_q % edge) // TW
    firsts = [min(max(half * span - 1, 0), groups - reach) for half in range(groups // span)]

    def over(far_t, far_h):
        near_t = 1 + 2 * far_t
        near_h = 1 + 2 * far_h
        per_col = near_t * TT * near_h * edge
        nk = reach * per_col
        q_col = lax.broadcasted_iota(jnp.int32, (nq, nk), 0) // (TT * edge)
        k_col = lax.broadcasted_iota(jnp.int32, (nq, nk), 1) // per_col
        for half, first in enumerate(firsts):
            gap = jnp.abs(q_col - k_col + (half * span - first))
            bias_ref[half, :, :nk] = jnp.where(gap <= rad_w, 0.0, NEG)
        at = lax.broadcasted_iota(jnp.int32, (1, nk), 1) % per_col
        k_frame = at // (near_h * edge)
        k_row = (at % (near_h * edge)) // TW

        @pl.loop(0, tiles_t * tiles_h)
        def _(step):
            th = step % tiles_h
            tt = step // tiles_h
            live_t = jnp.zeros((1, nk), jnp.int32)
            live_h = jnp.zeros((1, nk), jnp.int32)
            for near in range(near_t):
                count = info_ref[base_t + tt + 1 - far_t + near]
                live_t = jnp.where(k_frame // TT == near, count, live_t)
            for near in range(near_h):
                count = info_ref[base_h + th + 1 - far_h + near]
                live_h = jnp.where(k_row // TH == near, count, live_h)
            key_ok = (k_frame % TT < live_t) & (k_row % TH < live_h)
            key_bias = jnp.where(key_ok, 0.0, NEG)
            live = (q_frame < info_ref[base_t + tt + 1]) & (q_row < info_ref[base_h + th + 1])
            q_rows = pl.ds(pl.multiple_of(th * edge, edge), edge)
            k_rows = pl.ds(pl.multiple_of((th + 1 - far_h) * edge, edge), near_h * edge)
            q_frames = pl.ds(tt * TT, TT)
            k_frames = pl.ds((tt + 1 - far_t) * TT, near_t * TT)
            for half, first in enumerate(firsts):
                q_cols = slice(half * span, (half + 1) * span)
                k_cols = slice(first, first + reach)
                q = q_ref[q_cols, q_frames, q_rows, :].reshape(nq, head_dim)
                k = k_ref[k_cols, k_frames, k_rows, :].reshape(nk, head_dim)
                v = v_ref[k_cols, k_frames, k_rows, :].reshape(nk, head_dim)
                scores = lax.dot_general(
                    q, k, (((1,), (1,)), ((), ())), preferred_element_type=jnp.float32
                )
                scores = scores * scale + (bias_ref[half, :, :nk] + key_bias)
                top = jnp.max(scores, axis=1, keepdims=True)
                raised = jnp.exp2(scores - top)
                summed = jnp.sum(raised, axis=1, keepdims=True)
                blended = jnp.dot(
                    raised.astype(jnp.bfloat16), v, preferred_element_type=jnp.float32
                )
                result = jnp.where(live, blended / summed, 0.0).astype(jnp.bfloat16)
                out_ref[q_cols, here, q_frames, q_rows, :] = result.reshape(
                    span, TT, edge, head_dim
                )

    for far_t in (0, 1):
        for far_h in (0, 1):
            pl.when((rad_t == far_t) & (rad_h == far_h))(functools.partial(over, far_t, far_h))


def attend(info, pieces, queries, heads, head, slot, before, frames):
    groups, _, own, head_dim = queries.shape
    span = max(groups // 2, 1)
    reach = min(span + 1, groups)
    edge = TH * TW
    nq = span * TT * edge
    nk = reach * 9 * TT * edge
    steps = heads * (frames // TT) * (own // edge) * (groups // span)
    ext = (groups, frames + 2 * TT, own + 2 * edge, head_dim)
    in_specs = [pl.BlockSpec(memory_space=pltpu.SMEM)]
    in_specs += [
        pl.BlockSpec(
            (groups, 2 * sum(n for _, n in spans), a.shape[2], head_dim), lambda h: (0, h, 0, 0)
        )
        for a, spans, _ in pieces
    ]
    in_specs += [
        pl.BlockSpec((groups, frames, own, head_dim), lambda h: (0, head + h, 0, 0)),
    ]
    args = [info, *(a for a, _, _ in pieces), queries]
    total = slot + heads
    if before is not None:
        in_specs.append(pl.BlockSpec(before.shape, lambda h: (0, 0, 0, 0, 0)))
        args.append(before)
    return pl.pallas_call(
        functools.partial(
            attend_kernel,
            tuple((spans, low) for _, spans, low in pieces),
            frames,
            span,
            reach,
            math.log2(math.e) / math.sqrt(head_dim),
            head,
            slot,
        ),
        grid=(heads,),
        in_specs=in_specs,
        out_specs=pl.BlockSpec(memory_space=pltpu.VMEM),
        out_shape=pltpu.VMEM((groups, total, frames, own, head_dim), jnp.bfloat16),
        scratch_shapes=[
            pltpu.VMEM(ext, jnp.bfloat16),
            pltpu.VMEM(ext, jnp.bfloat16),
            pltpu.VMEM((groups // span, nq, nk), jnp.float32),
        ],
        cost_estimate=cost(4 * steps * nq * nk * head_dim, heads * (4 << 20), steps * nq * nk),
        compiler_params=pltpu.CompilerParams(vmem_limit_bytes=GRANT),
        name="attend",
    )(*args)


def unpack_kernel(order, in_ref, out_ref):
    frames, rows, cols = out_ref.shape[:3]
    groups, heads, _, _, head_dim = in_ref.shape
    for slot, head in enumerate(order):
        for group in range(groups):
            at = (heads * group + head) * head_dim
            x = in_ref[group, slot].astype(jnp.float32).reshape(frames, rows, cols, head_dim)
            out_ref[:, :, :, at : at + head_dim] = x.astype(jnp.bfloat16)


def unpack(value, order, rows, cols):
    groups, heads, frames, _, head_dim = value.shape
    out = (frames, rows, cols, groups * heads * head_dim)
    return pl.pallas_call(
        functools.partial(unpack_kernel, order),
        in_specs=[pl.BlockSpec(memory_space=pltpu.VMEM)],
        out_specs=pl.BlockSpec(memory_space=pltpu.VMEM),
        out_shape=jax.ShapeDtypeStruct(out, jnp.bfloat16),
        compiler_params=pltpu.CompilerParams(vmem_limit_bytes=16 << 20),
        name="unpack",
    )(value)


def shifted(value, axis, step):
    size = lax.axis_size(axis)
    pairs = [(i, i + 1) if step > 0 else (i + 1, i) for i in range(size - 1)]
    return lax.ppermute(value, axis, pairs)


def exchange(value):
    return lax.all_to_all(value, "hd", split_axis=0, concat_axis=0, tiled=True)


def shards(qkv, q_gain, k_gain, windows, frame_counts, row_counts):
    frames, rows, cols, channels = qkv.shape
    head_dim = q_gain.shape[0]
    groups = lax.axis_size("hd")
    heads = channels // (3 * head_dim) // groups
    edge = TH * TW
    own = rows * cols
    tiles_t = frames // TT
    tiles_h = rows // TH
    near_t = lax.dynamic_slice(
        jnp.pad(frame_counts, (1, 1)), (lax.axis_index("ta") * tiles_t,), (tiles_t + 2,)
    )
    near_h = lax.dynamic_slice(
        jnp.pad(row_counts, (1, 1)), (lax.axis_index("ha") * tiles_h,), (tiles_h + 2,)
    )
    info = jnp.concatenate([windows.reshape(-1), near_t, near_h])

    def packed(entries, tiles=False):
        return pack(qkv, q_gain, k_gain, tuple(entries), heads, groups, tiles)

    rest = heads - 1
    long = frames + 2 * TT
    value_z, first_z, last_z = packed([(1, rest), (2, rest)], True)
    tz0 = shifted(last_z, "ta", 1)
    tz1 = shifted(first_z, "ta", -1)
    value_n = packed([(part, head) for head in range(rest) for part in (1, 2)])
    got_n = exchange(value_n)
    got_q = exchange(packed([(0, head) for head in range(heads)]))
    joined = join(value_z, tz0, tz1)
    got_z = exchange(joined)

    first_n, last_n = tiles_of(got_n, frames)
    tn0 = shifted(last_n, "ta", 1)
    tn1 = shifted(first_n, "ta", -1)
    low_c, high_c = rim((got_n,), (frames,), 2 * rest, edge)
    hc0 = shifted(high_c, "ha", 1)
    hc1 = shifted(low_c, "ha", -1)
    low_z, high_z = rim((got_z,), (long,), 2, edge)
    hz0 = shifted(high_z, "ha", 1)
    hz1 = shifted(low_z, "ha", -1)
    low_t, high_t = rim((tn0, tn1), (TT, TT), 2 * rest, edge)
    ht0 = shifted(high_t, "ha", 1)
    ht1 = shifted(low_t, "ha", -1)

    mine, every = ((TT, frames),), ((0, long),)
    beside = ((0, TT), (TT + frames, TT))
    pieces_n = (
        (got_n, mine, edge),
        (tn0, ((0, TT),), edge),
        (tn1, ((TT + frames, TT),), edge),
        (hc0, mine, 0),
        (hc1, mine, edge + own),
        (ht0, beside, 0),
        (ht1, beside, edge + own),
    )
    pieces_z = ((got_z, every, edge), (hz0, every, 0), (hz1, every, edge + own))
    out = attend(info, pieces_z, got_q, 1, rest, 0, None, frames)
    out = attend(info, pieces_n, got_q, rest, 0, 1, out, frames)
    return unpack(exchange(out), (rest, *range(rest)), rows, cols)


def solution(mesh):
    return jax.shard_map(
        shards,
        mesh=mesh,
        in_specs=(P("ta", "ha", "hd", None), P(), P(), P("hd", None), P(), P()),
        out_specs=P("ta", "ha", "hd", None),
        check_vma=False,
    )
```

```python
import functools
import math

import jax
import jax.numpy as jnp
from jax import lax
from jax.experimental import pallas as pl
from jax.experimental.pallas import tpu as pltpu
from jax.sharding import PartitionSpec as P


TT = 2
TH = 2
TW = 8
NEG = -1e30

GRANT = 24 << 20
PACK_GRANT = 62 << 20


def cost(flops, size, transcendentals=0):
    return pl.CostEstimate(flops=flops, bytes_accessed=size, transcendentals=transcendentals)


def pack_kernel(entries, parts, heads_local, tiles, *refs):
    part_refs = refs[: len(parts)]
    qg_ref, kg_ref, out_ref = refs[len(parts) : len(parts) + 3]
    rim_refs = refs[len(parts) + 3 :]
    frames, rows, cols = part_refs[0].shape[:3]
    groups = out_ref.shape[0]
    head_dim = qg_ref.shape[-1]
    gains = {0: qg_ref[...].reshape(1, 1, 1, head_dim), 1: kg_ref[...].reshape(1, 1, 1, head_dim)}
    for dest in range(groups):
        for slot, (part, head) in enumerate(entries):
            at = (heads_local * dest + head) * head_dim
            x = part_refs[parts.index(part)][:, :, :, at : at + head_dim].astype(jnp.float32)
            if part in gains:
                meansq = jnp.mean(x * x, axis=-1, keepdims=True)
                x = x * lax.rsqrt(meansq + 1e-06) * gains[part]
            x = x.reshape(frames, rows * cols, head_dim).astype(jnp.bfloat16)
            out_ref[dest, slot * frames : (slot + 1) * frames] = x
            if tiles:
                rim_refs[0][dest, slot * TT : (slot + 1) * TT] = x[:TT]
                rim_refs[1][dest, slot * TT : (slot + 1) * TT] = x[frames - TT :]


def whole(shape):
    return pl.BlockSpec(shape, lambda i: (0,) * len(shape))


def one_step(kernel, in_specs, outs, size, grant=None):
    shapes = [jax.ShapeDtypeStruct(shape, jnp.bfloat16) for shape in outs]
    return pl.pallas_call(
        kernel,
        grid=(1,),
        in_specs=in_specs,
        out_specs=[whole(shape) for shape in outs],
        out_shape=shapes,
        cost_estimate=cost(size, size),
        compiler_params=pltpu.CompilerParams(vmem_limit_bytes=grant or GRANT),
    )


def pack(qkv, q_gain, k_gain, entries, heads_local, groups, tiles=False):
    frames, rows, cols, channels = qkv.shape
    head_dim = q_gain.shape[-1]
    third = channels // 3
    parts = sorted({part for part, _ in entries})
    n = len(entries)
    own = rows * cols
    outs = [(groups, n * frames, own, head_dim)] + [(groups, n * TT, own, head_dim)] * (2 * tiles)
    in_specs = [
        pl.BlockSpec((frames, rows, cols, third), functools.partial(lambda p, i: (0, 0, 0, p), part))
        for part in parts
    ] + [whole((1, head_dim))] * 2
    kernel = functools.partial(pack_kernel, entries, parts, heads_local, tiles)
    packed = one_step(kernel, in_specs, outs, 4 * math.prod(outs[0]), PACK_GRANT)(
        *([qkv] * len(parts)), q_gain.reshape(1, -1), k_gain.reshape(1, -1)
    )
    return packed if tiles else packed[0]


def pack_shifts_kernel(heads, groups, me_ref, part_ref, gain_ref, *out_refs):
    frames, rows, cols = part_ref.shape[:3]
    head_dim = gain_ref.shape[-1]
    gain = gain_ref[...].reshape(1, 1, 1, head_dim)
    for shift in range(groups):
        dest = lax.rem(me_ref[0] + shift, groups)
        for head in range(heads):
            at = pl.multiple_of((heads * dest + head) * head_dim, head_dim)
            x = part_ref[:, :, :, pl.ds(at, head_dim)].astype(jnp.float32)
            meansq = jnp.mean(x * x, axis=-1, keepdims=True)
            x = x * lax.rsqrt(meansq + 1e-06) * gain
            x = x.reshape(frames, rows * cols, head_dim).astype(jnp.bfloat16)
            out_refs[shift][head * frames : (head + 1) * frames] = x


def pack_shifts(me, qkv, gain, heads, groups):
    frames, rows, cols, channels = qkv.shape
    head_dim = gain.shape[-1]
    outs = [(heads * frames, rows * cols, head_dim)] * groups
    return one_step(
        functools.partial(pack_shifts_kernel, heads, groups),
        [
            pl.BlockSpec(memory_space=pltpu.SMEM),
            pl.BlockSpec((frames, rows, cols, channels // 3), lambda i: (0, 0, 0, 0)),
            whole((1, head_dim)),
        ],
        outs,
        4 * groups * math.prod(outs[0]),
        PACK_GRANT,
    )(me, qkv, gain.reshape(1, -1))


def join_kernel(frames, c_ref, t0_ref, t1_ref, out_ref):
    long = frames + 2 * TT
    for kv in range(2):
        at = kv * long
        out_ref[:, at : at + TT] = t0_ref[:, kv * TT : (kv + 1) * TT]
        out_ref[:, at + TT : at + TT + frames] = c_ref[:, kv * frames : (kv + 1) * frames]
        out_ref[:, at + TT + frames : at + long] = t1_ref[:, kv * TT : (kv + 1) * TT]


def join(center, t0, t1):
    groups, slabs, own, head_dim = center.shape
    frames = slabs // 2
    total = 2 * (frames + 2 * TT)
    arrays = (center, t0, t1)
    out = (groups, total, own, head_dim)
    return one_step(
        functools.partial(join_kernel, frames),
        [whole(a.shape) for a in arrays],
        [out],
        4 * math.prod(out),
        PACK_GRANT,
    )(*arrays)[0]


def tiles_kernel(frames, ref, first_ref, last_ref):
    for n in range(ref.shape[1] // frames):
        to = slice(n * TT, (n + 1) * TT)
        first_ref[:, to] = ref[:, n * frames : n * frames + TT]
        last_ref[:, to] = ref[:, (n + 1) * frames - TT : (n + 1) * frames]


def tiles_of(value, frames):
    groups, slabs, own, head_dim = value.shape
    out = (groups, slabs // frames * TT, own, head_dim)
    return one_step(
        functools.partial(tiles_kernel, frames),
        [whole(value.shape)],
        [out, out],
        8 * math.prod(out),
    )(value)


def rim_kernel(edge, counts, *refs):
    low_ref, high_ref = refs[-2:]
    sources = refs[:-2]
    own = sources[0].shape[2]
    total = sum(counts)
    for n in range(low_ref.shape[1] // total):
        at = n * total
        for ref, count in zip(sources, counts):
            src = slice(n * count, (n + 1) * count)
            low_ref[:, at : at + count] = ref[:, src, 0:edge]
            high_ref[:, at : at + count] = ref[:, src, own - edge : own]
            at += count


def rim(arrays, counts, heads, edge):
    groups, _, own, head_dim = arrays[0].shape
    out = (groups, heads * sum(counts), edge, head_dim)
    in_specs = [whole((groups, heads * c, own, head_dim)) for c in counts]
    return one_step(
        functools.partial(rim_kernel, edge, counts), in_specs, [out, out], 8 * math.prod(out)
    )(*arrays)


def attend_kernel(pieces, frames, span, reach, scale, head, slot, info_ref, *refs):
    count = len(pieces)
    piece_refs = refs[:count]
    out_ref, k_ref, v_ref, q_ref, bias_ref = refs[-5:]
    groups = q_ref.shape[0]
    here = slot + pl.program_id(0)
    if slot:
        out_ref[:, 0:slot] = refs[count + groups][...]
    own, head_dim = q_ref.shape[2:]
    edge = TH * TW
    for ref, (spans, low) in zip(piece_refs, pieces):
        tokens = slice(low, low + ref.shape[2])
        at = 0
        for dst in (k_ref, v_ref):
            for start, n in spans:
                dst[:, start : start + n, tokens] = ref[:, at : at + n]
                at += n

    tiles_t = frames // TT
    tiles_h = own // edge
    base_t = info_ref.shape[0] - (tiles_t + 2) - (tiles_h + 2)
    base_h = base_t + tiles_t + 2
    for shift in range(groups):
        q_ref[lax.rem(info_ref[base_t - 1] + (groups - shift), groups)] = refs[count + shift][...]
    head = head + pl.program_id(0)
    rad_t = info_ref[3 * head]
    rad_h = info_ref[3 * head + 1]
    rad_w = info_ref[3 * head + 2]
    nq = span * TT * edge
    at_q = lax.broadcasted_iota(jnp.int32, (nq, 1), 0) % (TT * edge)
    q_frame = at_q // edge
    q_row = (at_q % edge) // TW
    firsts = [min(max(half * span - 1, 0), groups - reach) for half in range(groups // span)]

    def over(far_t, far_h):
        near_t = 1 + 2 * far_t
        near_h = 1 + 2 * far_h
        per_col = near_t * TT * near_h * edge
        nk = reach * per_col
        q_col = lax.broadcasted_iota(jnp.int32, (nq, nk), 0) // (TT * edge)
        k_col = lax.broadcasted_iota(jnp.int32, (nq, nk), 1) // per_col
        for half, first in enumerate(firsts):
            gap = jnp.abs(q_col - k_col + (half * span - first))
            bias_ref[half, :, :nk] = jnp.where(gap <= rad_w, 0.0, NEG)
        at = lax.broadcasted_iota(jnp.int32, (1, nk), 1) % per_col
        k_frame = at // (near_h * edge)
        k_row = (at % (near_h * edge)) // TW

        @pl.loop(0, tiles_t * tiles_h)
        def _(step):
            th = step % tiles_h
            tt = step // tiles_h
            live_t = jnp.zeros((1, nk), jnp.int32)
            live_h = jnp.zeros((1, nk), jnp.int32)
            for near in range(near_t):
                count = info_ref[base_t + tt + 1 - far_t + near]
                live_t = jnp.where(k_frame // TT == near, count, live_t)
            for near in range(near_h):
                count = info_ref[base_h + th + 1 - far_h + near]
                live_h = jnp.where(k_row // TH == near, count, live_h)
            key_ok = (k_frame % TT < live_t) & (k_row % TH < live_h)
            key_bias = jnp.where(key_ok, 0.0, NEG)
            live = (q_frame < info_ref[base_t + tt + 1]) & (q_row < info_ref[base_h + th + 1])
            q_rows = pl.ds(pl.multiple_of(th * edge, edge), edge)
            k_rows = pl.ds(pl.multiple_of((th + 1 - far_h) * edge, edge), near_h * edge)
            q_frames = pl.ds(tt * TT, TT)
            k_frames = pl.ds((tt + 1 - far_t) * TT, near_t * TT)
            for half, first in enumerate(firsts):
                q_cols = slice(half * span, (half + 1) * span)
                k_cols = slice(first, first + reach)
                q = q_ref[q_cols, q_frames, q_rows, :].reshape(nq, head_dim)
                k = k_ref[k_cols, k_frames, k_rows, :].reshape(nk, head_dim)
                v = v_ref[k_cols, k_frames, k_rows, :].reshape(nk, head_dim)
                scores = lax.dot_general(
                    q, k, (((1,), (1,)), ((), ())), preferred_element_type=jnp.float32
                )
                scores = scores * scale + (bias_ref[half, :, :nk] + key_bias)
                top = jnp.max(scores, axis=1, keepdims=True)
                raised = jnp.exp2(scores - top)
                summed = jnp.sum(raised, axis=1, keepdims=True)
                blended = jnp.dot(
                    raised.astype(jnp.bfloat16), v, preferred_element_type=jnp.float32
                )
                result = jnp.where(live, blended / summed, 0.0).astype(jnp.bfloat16)
                out_ref[q_cols, here, q_frames, q_rows, :] = result.reshape(
                    span, TT, edge, head_dim
                )

    for far_t in (0, 1):
        for far_h in (0, 1):
            pl.when((rad_t == far_t) & (rad_h == far_h))(functools.partial(over, far_t, far_h))


def attend(info, pieces, queries, heads, head, slot, before, frames):
    groups = len(queries)
    _, own, head_dim = queries[0].shape
    span = max(groups // 2, 1)
    reach = min(span + 1, groups)
    edge = TH * TW
    nq = span * TT * edge
    nk = reach * 9 * TT * edge
    steps = heads * (frames // TT) * (own // edge) * (groups // span)
    ext = (groups, frames + 2 * TT, own + 2 * edge, head_dim)
    in_specs = [pl.BlockSpec(memory_space=pltpu.SMEM)]
    in_specs += [
        pl.BlockSpec(
            (groups, 2 * sum(n for _, n in spans), a.shape[2], head_dim), lambda h: (0, h, 0, 0)
        )
        for a, spans, _ in pieces
    ]
    in_specs += [
        pl.BlockSpec((frames, own, head_dim), lambda h: (head + h, 0, 0)) for _ in queries
    ]
    args = [info, *(a for a, _, _ in pieces), *queries]
    total = slot + heads
    if before is not None:
        in_specs.append(pl.BlockSpec(before.shape, lambda h: (0, 0, 0, 0, 0)))
        args.append(before)
    return pl.pallas_call(
        functools.partial(
            attend_kernel,
            tuple((spans, low) for _, spans, low in pieces),
            frames,
            span,
            reach,
            math.log2(math.e) / math.sqrt(head_dim),
            head,
            slot,
        ),
        grid=(heads,),
        in_specs=in_specs,
        out_specs=pl.BlockSpec(memory_space=pltpu.VMEM),
        out_shape=pltpu.VMEM((groups, total, frames, own, head_dim), jnp.bfloat16),
        scratch_shapes=[
            pltpu.VMEM(ext, jnp.bfloat16),
            pltpu.VMEM(ext, jnp.bfloat16),
            pltpu.VMEM((groups, frames, own, head_dim), jnp.bfloat16),
            pltpu.VMEM((groups // span, nq, nk), jnp.float32),
        ],
        cost_estimate=cost(4 * steps * nq * nk * head_dim, heads * (4 << 20), steps * nq * nk),
        compiler_params=pltpu.CompilerParams(vmem_limit_bytes=GRANT),
        name="attend",
    )(*args)


def unpack_kernel(order, in_ref, out_ref):
    frames, rows, cols = out_ref.shape[:3]
    groups, heads, _, _, head_dim = in_ref.shape
    for slot, head in enumerate(order):
        for group in range(groups):
            at = (heads * group + head) * head_dim
            x = in_ref[group, slot].astype(jnp.float32).reshape(frames, rows, cols, head_dim)
            out_ref[:, :, :, at : at + head_dim] = x.astype(jnp.bfloat16)


def unpack(value, order, rows, cols):
    groups, heads, frames, _, head_dim = value.shape
    out = (frames, rows, cols, groups * heads * head_dim)
    return pl.pallas_call(
        functools.partial(unpack_kernel, order),
        in_specs=[pl.BlockSpec(memory_space=pltpu.VMEM)],
        out_specs=pl.BlockSpec(memory_space=pltpu.VMEM),
        out_shape=jax.ShapeDtypeStruct(out, jnp.bfloat16),
        compiler_params=pltpu.CompilerParams(vmem_limit_bytes=16 << 20),
        name="unpack",
    )(value)


def shifted(value, axis, step):
    size = lax.axis_size(axis)
    pairs = [(i, i + 1) if step > 0 else (i + 1, i) for i in range(size - 1)]
    return lax.ppermute(value, axis, pairs)


def exchange(value):
    return lax.all_to_all(value, "hd", split_axis=0, concat_axis=0, tiled=True)


def shards(qkv, q_gain, k_gain, windows, frame_counts, row_counts):
    frames, rows, cols, channels = qkv.shape
    head_dim = q_gain.shape[0]
    groups = lax.axis_size("hd")
    heads = channels // (3 * head_dim) // groups
    edge = TH * TW
    own = rows * cols
    tiles_t = frames // TT
    tiles_h = rows // TH
    me = lax.axis_index("hd").astype(jnp.int32).reshape(1)
    near_t = lax.dynamic_slice(
        jnp.pad(frame_counts, (1, 1)), (lax.axis_index("ta") * tiles_t,), (tiles_t + 2,)
    )
    near_h = lax.dynamic_slice(
        jnp.pad(row_counts, (1, 1)), (lax.axis_index("ha") * tiles_h,), (tiles_h + 2,)
    )
    info = jnp.concatenate([windows.reshape(-1), me, near_t, near_h])

    def packed(entries, tiles=False):
        return pack(qkv, q_gain, k_gain, tuple(entries), heads, groups, tiles)

    rest = heads - 1
    long = frames + 2 * TT
    value_z, first_z, last_z = packed([(1, rest), (2, rest)], True)
    tz0 = shifted(last_z, "ta", 1)
    tz1 = shifted(first_z, "ta", -1)
    value_n = packed([(part, head) for head in range(rest) for part in (1, 2)])
    got_n = exchange(value_n)
    value_q = pack_shifts(me, qkv, q_gain, heads, groups)
    got_q = list(value_q[:1])
    for shift in range(1, groups):
        hops = [(i, (i + shift) % groups) for i in range(groups)]
        got_q.append(lax.ppermute(value_q[shift], "hd", hops))
    joined = join(value_z, tz0, tz1)
    got_z = exchange(joined)

    first_n, last_n = tiles_of(got_n, frames)
    tn0 = shifted(last_n, "ta", 1)
    tn1 = shifted(first_n, "ta", -1)
    low_c, high_c = rim((got_n,), (frames,), 2 * rest, edge)
    hc0 = shifted(high_c, "ha", 1)
    hc1 = shifted(low_c, "ha", -1)
    low_z, high_z = rim((got_z,), (long,), 2, edge)
    hz0 = shifted(high_z, "ha", 1)
    hz1 = shifted(low_z, "ha", -1)
    low_t, high_t = rim((tn0, tn1), (TT, TT), 2 * rest, edge)
    ht0 = shifted(high_t, "ha", 1)
    ht1 = shifted(low_t, "ha", -1)

    mine, every = ((TT, frames),), ((0, long),)
    beside = ((0, TT), (TT + frames, TT))
    pieces_n = (
        (got_n, mine, edge),
        (tn0, ((0, TT),), edge),
        (tn1, ((TT + frames, TT),), edge),
        (hc0, mine, 0),
        (hc1, mine, edge + own),
        (ht0, beside, 0),
        (ht1, beside, edge + own),
    )
    pieces_z = ((got_z, every, edge), (hz0, every, 0), (hz1, every, edge + own))
    out = attend(info, pieces_z, got_q, 1, rest, 0, None, frames)
    out = attend(info, pieces_n, got_q, rest, 0, 1, out, frames)
    return unpack(exchange(out), (rest, *range(rest)), rows, cols)


def solution(mesh):
    return jax.shard_map(
        shards,
        mesh=mesh,
        in_specs=(P("ta", "ha", "hd", None), P(), P(), P("hd", None), P(), P()),
        out_specs=P("ta", "ha", "hd", None),
        check_vma=False,
    )
```

```python
import functools
import math

import jax
import jax.numpy as jnp
from jax import lax
from jax.experimental import pallas as pl
from jax.experimental.pallas import tpu as pltpu
from jax.sharding import PartitionSpec as P


TT = 2
TH = 2
TW = 8
NEG = -1e30

GRANT = 24 << 20
PACK_GRANT = 62 << 20


def cost(flops, size, transcendentals=0):
    return pl.CostEstimate(flops=flops, bytes_accessed=size, transcendentals=transcendentals)


def pack_kernel(entries, parts, heads_local, tiles, *refs):
    part_refs = refs[: len(parts)]
    qg_ref, kg_ref, out_ref = refs[len(parts) : len(parts) + 3]
    rim_refs = refs[len(parts) + 3 :]
    frames, rows, cols = part_refs[0].shape[:3]
    groups = out_ref.shape[0]
    head_dim = qg_ref.shape[-1]
    gains = {0: qg_ref[...].reshape(1, 1, 1, head_dim), 1: kg_ref[...].reshape(1, 1, 1, head_dim)}
    for dest in range(groups):
        for slot, (part, head) in enumerate(entries):
            at = (heads_local * dest + head) * head_dim
            x = part_refs[parts.index(part)][:, :, :, at : at + head_dim].astype(jnp.float32)
            if part in gains:
                meansq = jnp.mean(x * x, axis=-1, keepdims=True)
                x = x * lax.rsqrt(meansq + 1e-06) * gains[part]
            x = x.reshape(frames, rows * cols, head_dim).astype(jnp.bfloat16)
            out_ref[dest, slot * frames : (slot + 1) * frames] = x
            if tiles:
                rim_refs[0][dest, slot * TT : (slot + 1) * TT] = x[:TT]
                rim_refs[1][dest, slot * TT : (slot + 1) * TT] = x[frames - TT :]


def whole(shape):
    return pl.BlockSpec(shape, lambda i: (0,) * len(shape))


def one_step(kernel, in_specs, outs, size, grant=None):
    shapes = [jax.ShapeDtypeStruct(shape, jnp.bfloat16) for shape in outs]
    return pl.pallas_call(
        kernel,
        grid=(1,),
        in_specs=in_specs,
        out_specs=[whole(shape) for shape in outs],
        out_shape=shapes,
        cost_estimate=cost(size, size),
        compiler_params=pltpu.CompilerParams(vmem_limit_bytes=grant or GRANT),
    )


def pack(qkv, q_gain, k_gain, entries, heads_local, groups, tiles=False):
    frames, rows, cols, channels = qkv.shape
    head_dim = q_gain.shape[-1]
    third = channels // 3
    parts = sorted({part for part, _ in entries})
    n = len(entries)
    own = rows * cols
    outs = [(groups, n * frames, own, head_dim)] + [(groups, n * TT, own, head_dim)] * (2 * tiles)
    in_specs = [
        pl.BlockSpec((frames, rows, cols, third), functools.partial(lambda p, i: (0, 0, 0, p), part))
        for part in parts
    ] + [whole((1, head_dim))] * 2
    kernel = functools.partial(pack_kernel, entries, parts, heads_local, tiles)
    packed = one_step(kernel, in_specs, outs, 4 * math.prod(outs[0]), PACK_GRANT)(
        *([qkv] * len(parts)), q_gain.reshape(1, -1), k_gain.reshape(1, -1)
    )
    return packed if tiles else packed[0]


def join_kernel(frames, c_ref, t0_ref, t1_ref, q_ref, out_ref):
    long = frames + 2 * TT
    for kv in range(2):
        at = kv * long
        out_ref[:, at : at + TT] = t0_ref[:, kv * TT : (kv + 1) * TT]
        out_ref[:, at + TT : at + TT + frames] = c_ref[:, kv * frames : (kv + 1) * frames]
        out_ref[:, at + TT + frames : at + long] = t1_ref[:, kv * TT : (kv + 1) * TT]
    out_ref[:, 2 * long :] = q_ref[...]


def join(center, t0, t1, queries):
    groups, slabs, own, head_dim = center.shape
    frames = slabs // 2
    total = 2 * (frames + 2 * TT) + queries.shape[1]
    arrays = (center, t0, t1, queries)
    out = (groups, total, own, head_dim)
    return one_step(
        functools.partial(join_kernel, frames),
        [whole(a.shape) for a in arrays],
        [out],
        4 * math.prod(out),
        PACK_GRANT,
    )(*arrays)[0]


def tiles_kernel(frames, ref, first_ref, last_ref):
    for n in range(first_ref.shape[1] // TT):
        to = slice(n * TT, (n + 1) * TT)
        first_ref[:, to] = ref[:, n * frames : n * frames + TT]
        last_ref[:, to] = ref[:, (n + 1) * frames - TT : (n + 1) * frames]


def tiles_of(value, slabs, frames):
    groups, _, own, head_dim = value.shape
    out = (groups, slabs // frames * TT, own, head_dim)
    return one_step(
        functools.partial(tiles_kernel, frames),
        [whole((groups, slabs, own, head_dim))],
        [out, out],
        8 * math.prod(out),
    )(value)


def rim_kernel(edge, counts, *refs):
    low_ref, high_ref = refs[-2:]
    sources = refs[:-2]
    own = sources[0].shape[2]
    total = sum(counts)
    for n in range(low_ref.shape[1] // total):
        at = n * total
        for ref, count in zip(sources, counts):
            src = slice(n * count, (n + 1) * count)
            low_ref[:, at : at + count] = ref[:, src, 0:edge]
            high_ref[:, at : at + count] = ref[:, src, own - edge : own]
            at += count


def rim(arrays, counts, heads, edge):
    groups, _, own, head_dim = arrays[0].shape
    out = (groups, heads * sum(counts), edge, head_dim)
    in_specs = [whole((groups, heads * c, own, head_dim)) for c in counts]
    return one_step(
        functools.partial(rim_kernel, edge, counts), in_specs, [out, out], 8 * math.prod(out)
    )(*arrays)


def attend_kernel(pieces, frames, span, reach, scale, head, slot, info_ref, *refs):
    count = len(pieces)
    piece_refs = refs[:count]
    q_ref = refs[count]
    out_ref, k_ref, v_ref, bias_ref = refs[-4:]
    here = slot + pl.program_id(0)
    if len(refs) > count + 5:
        out_ref[:, 0:slot] = refs[count + 1][...]
    groups = q_ref.shape[0]
    own, head_dim = q_ref.shape[2:]
    edge = TH * TW
    for ref, (spans, low) in zip(piece_refs, pieces):
        tokens = slice(low, low + ref.shape[2])
        at = 0
        for dst in (k_ref, v_ref):
            for start, n in spans:
                dst[:, start : start + n, tokens] = ref[:, at : at + n]
                at += n

    tiles_t = frames // TT
    tiles_h = own // edge
    base_t = info_ref.shape[0] - (tiles_t + 2) - (tiles_h + 2)
    base_h = base_t + tiles_t + 2
    head = head + pl.program_id(0)
    rad_t = info_ref[3 * head]
    rad_h = info_ref[3 * head + 1]
    rad_w = info_ref[3 * head + 2]
    nq = span * TT * edge
    at_q = lax.broadcasted_iota(jnp.int32, (nq, 1), 0) % (TT * edge)
    q_frame = at_q // edge
    q_row = (at_q % edge) // TW
    firsts = [min(max(half * span - 1, 0), groups - reach) for half in range(groups // span)]

    def over(far_t, far_h):
        near_t = 1 + 2 * far_t
        near_h = 1 + 2 * far_h
        per_col = near_t * TT * near_h * edge
        nk = reach * per_col
        q_col = lax.broadcasted_iota(jnp.int32, (nq, nk), 0) // (TT * edge)
        k_col = lax.broadcasted_iota(jnp.int32, (nq, nk), 1) // per_col
        for half, first in enumerate(firsts):
            gap = jnp.abs(q_col - k_col + (half * span - first))
            bias_ref[half, :, :nk] = jnp.where(gap <= rad_w, 0.0, NEG)
        at = lax.broadcasted_iota(jnp.int32, (1, nk), 1) % per_col
        k_frame = at // (near_h * edge)
        k_row = (at % (near_h * edge)) // TW

        @pl.loop(0, tiles_t * tiles_h)
        def _(step):
            th = step % tiles_h
            tt = step // tiles_h
            live_t = jnp.zeros((1, nk), jnp.int32)
            live_h = jnp.zeros((1, nk), jnp.int32)
            for near in range(near_t):
                count = info_ref[base_t + tt + 1 - far_t + near]
                live_t = jnp.where(k_frame // TT == near, count, live_t)
            for near in range(near_h):
                count = info_ref[base_h + th + 1 - far_h + near]
                live_h = jnp.where(k_row // TH == near, count, live_h)
            key_ok = (k_frame % TT < live_t) & (k_row % TH < live_h)
            key_bias = jnp.where(key_ok, 0.0, NEG)
            live = (q_frame < info_ref[base_t + tt + 1]) & (q_row < info_ref[base_h + th + 1])
            q_rows = pl.ds(pl.multiple_of(th * edge, edge), edge)
            k_rows = pl.ds(pl.multiple_of((th + 1 - far_h) * edge, edge), near_h * edge)
            q_frames = pl.ds(tt * TT, TT)
            k_frames = pl.ds((tt + 1 - far_t) * TT, near_t * TT)
            for half, first in enumerate(firsts):
                q_cols = slice(half * span, (half + 1) * span)
                k_cols = slice(first, first + reach)
                q = q_ref[q_cols, q_frames, q_rows, :].reshape(nq, head_dim)
                k = k_ref[k_cols, k_frames, k_rows, :].reshape(nk, head_dim)
                v = v_ref[k_cols, k_frames, k_rows, :].reshape(nk, head_dim)
                scores = lax.dot_general(
                    q, k, (((1,), (1,)), ((), ())), preferred_element_type=jnp.float32
                )
                scores = scores * scale + (bias_ref[half, :, :nk] + key_bias)
                top = jnp.max(scores, axis=1, keepdims=True)
                raised = jnp.exp2(scores - top)
                summed = jnp.sum(raised, axis=1, keepdims=True)
                blended = jnp.dot(
                    raised.astype(jnp.bfloat16), v, preferred_element_type=jnp.float32
                )
                result = jnp.where(live, blended / summed, 0.0).astype(jnp.bfloat16)
                out_ref[q_cols, here, q_frames, q_rows, :] = result.reshape(
                    span, TT, edge, head_dim
                )

    for far_t in (0, 1):
        for far_h in (0, 1):
            pl.when((rad_t == far_t) & (rad_h == far_h))(functools.partial(over, far_t, far_h))


def attend(info, pieces, queries, q_block, heads, head, slot, before, frames):
    groups, _, own, head_dim = queries.shape
    span = max(groups // 2, 1)
    reach = min(span + 1, groups)
    edge = TH * TW
    nq = span * TT * edge
    nk = reach * 9 * TT * edge
    steps = heads * (frames // TT) * (own // edge) * (groups // span)
    ext = (groups, frames + 2 * TT, own + 2 * edge, head_dim)
    in_specs = [pl.BlockSpec(memory_space=pltpu.SMEM)]
    in_specs += [
        pl.BlockSpec(
            (groups, 2 * sum(n for _, n in spans), a.shape[2], head_dim), lambda h: (0, h, 0, 0)
        )
        for a, spans, _ in pieces
    ]
    in_specs += [
        pl.BlockSpec((groups, frames, own, head_dim), lambda h: (0, q_block + h, 0, 0)),
    ]
    args = [info, *(a for a, _, _ in pieces), queries]
    total = slot + heads
    if before is not None:
        in_specs.append(pl.BlockSpec(before.shape, lambda h: (0, 0, 0, 0, 0)))
        args.append(before)
    return pl.pallas_call(
        functools.partial(
            attend_kernel,
            tuple((spans, low) for _, spans, low in pieces),
            frames,
            span,
            reach,
            math.log2(math.e) / math.sqrt(head_dim),
            head,
            slot,
        ),
        grid=(heads,),
        in_specs=in_specs,
        out_specs=pl.BlockSpec(memory_space=pltpu.VMEM),
        out_shape=pltpu.VMEM((groups, total, frames, own, head_dim), jnp.bfloat16),
        scratch_shapes=[
            pltpu.VMEM(ext, jnp.bfloat16),
            pltpu.VMEM(ext, jnp.bfloat16),
            pltpu.VMEM((groups // span, nq, nk), jnp.float32),
        ],
        cost_estimate=cost(4 * steps * nq * nk * head_dim, heads * (4 << 20), steps * nq * nk),
        compiler_params=pltpu.CompilerParams(vmem_limit_bytes=GRANT),
        name="attend",
    )(*args)


def unpack_kernel(order, in_ref, out_ref):
    frames, rows, cols = out_ref.shape[:3]
    groups, heads, _, _, head_dim = in_ref.shape
    for slot, head in enumerate(order):
        for group in range(groups):
            at = (heads * group + head) * head_dim
            x = in_ref[group, slot].astype(jnp.float32).reshape(frames, rows, cols, head_dim)
            out_ref[:, :, :, at : at + head_dim] = x.astype(jnp.bfloat16)


def unpack(value, order, rows, cols):
    groups, heads, frames, _, head_dim = value.shape
    out = (frames, rows, cols, groups * heads * head_dim)
    return pl.pallas_call(
        functools.partial(unpack_kernel, order),
        in_specs=[pl.BlockSpec(memory_space=pltpu.VMEM)],
        out_specs=pl.BlockSpec(memory_space=pltpu.VMEM),
        out_shape=jax.ShapeDtypeStruct(out, jnp.bfloat16),
        compiler_params=pltpu.CompilerParams(vmem_limit_bytes=16 << 20),
        name="unpack",
    )(value)


def shifted(value, axis, step):
    size = lax.axis_size(axis)
    pairs = [(i, i + 1) if step > 0 else (i + 1, i) for i in range(size - 1)]
    return lax.ppermute(value, axis, pairs)


def exchange(value):
    return lax.all_to_all(value, "hd", split_axis=0, concat_axis=0, tiled=True)


def shards(qkv, q_gain, k_gain, windows, frame_counts, row_counts):
    frames, rows, cols, channels = qkv.shape
    head_dim = q_gain.shape[0]
    groups = lax.axis_size("hd")
    heads = channels // (3 * head_dim) // groups
    edge = TH * TW
    own = rows * cols
    tiles_t = frames // TT
    tiles_h = rows // TH
    near_t = lax.dynamic_slice(
        jnp.pad(frame_counts, (1, 1)), (lax.axis_index("ta") * tiles_t,), (tiles_t + 2,)
    )
    near_h = lax.dynamic_slice(
        jnp.pad(row_counts, (1, 1)), (lax.axis_index("ha") * tiles_h,), (tiles_h + 2,)
    )
    info = jnp.concatenate([windows.reshape(-1), near_t, near_h])

    def packed(entries, tiles=False):
        return pack(qkv, q_gain, k_gain, tuple(entries), heads, groups, tiles)

    rest = heads - 1
    long = frames + 2 * TT
    value_z, first_z, last_z = packed([(1, rest), (2, rest)], True)
    tz0 = shifted(last_z, "ta", 1)
    tz1 = shifted(first_z, "ta", -1)
    entries_n = [(part, head) for head in range(rest) for part in (1, 2)]
    value_n = packed([*entries_n, (0, rest)])
    got_n = exchange(value_n)
    value_q = packed([(0, head) for head in range(rest)])
    joined = join(value_z, tz0, tz1, value_q)
    got_z = exchange(joined)

    first_n, last_n = tiles_of(got_n, 2 * rest * frames, frames)
    tn0 = shifted(last_n, "ta", 1)
    tn1 = shifted(first_n, "ta", -1)
    low_c, high_c = rim((got_n,), (frames,), 2 * rest, edge)
    hc0 = shifted(high_c, "ha", 1)
    hc1 = shifted(low_c, "ha", -1)
    low_z, high_z = rim((got_z,), (long,), 2, edge)
    hz0 = shifted(high_z, "ha", 1)
    hz1 = shifted(low_z, "ha", -1)
    low_t, high_t = rim((tn0, tn1), (TT, TT), 2 * rest, edge)
    ht0 = shifted(high_t, "ha", 1)
    ht1 = shifted(low_t, "ha", -1)

    mine, every = ((TT, frames),), ((0, long),)
    beside = ((0, TT), (TT + frames, TT))
    pieces_n = (
        (got_n, mine, edge),
        (tn0, ((0, TT),), edge),
        (tn1, ((TT + frames, TT),), edge),
        (hc0, mine, 0),
        (hc1, mine, edge + own),
        (ht0, beside, 0),
        (ht1, beside, edge + own),
    )
    pieces_z = ((got_z, every, edge), (hz0, every, 0), (hz1, every, edge + own))
    out = attend(info, pieces_z, got_n, 2 * rest, 1, rest, 0, None, frames)
    out = attend(info, pieces_n, got_z, 2 * long // frames, rest, 0, 1, out, frames)
    return unpack(exchange(out), (rest, *range(rest)), rows, cols)


def solution(mesh):
    return jax.shard_map(
        shards,
        mesh=mesh,
        in_specs=(P("ta", "ha", "hd", None), P(), P(), P("hd", None), P(), P()),
        out_specs=P("ta", "ha", "hd", None),
        check_vma=False,
    )
```

```python
import functools
import math

import jax
import jax.numpy as jnp
from jax import lax
from jax.experimental import pallas as pl
from jax.experimental.pallas import tpu as pltpu
from jax.sharding import PartitionSpec as P


TT = 2
TH = 2
TW = 8
NEG = -1e30

GRANT = 24 << 20
PACK_GRANT = 62 << 20


def cost(flops, size, transcendentals=0):
    return pl.CostEstimate(flops=flops, bytes_accessed=size, transcendentals=transcendentals)


def pack_kernel(entries, parts, heads_local, tiles, *refs):
    part_refs = refs[: len(parts)]
    qg_ref, kg_ref, out_ref = refs[len(parts) : len(parts) + 3]
    rim_refs = refs[len(parts) + 3 :]
    frames, rows, cols = part_refs[0].shape[:3]
    groups = out_ref.shape[0]
    head_dim = qg_ref.shape[-1]
    gains = {0: qg_ref[...].reshape(1, 1, 1, head_dim), 1: kg_ref[...].reshape(1, 1, 1, head_dim)}
    for dest in range(groups):
        for slot, (part, head) in enumerate(entries):
            at = (heads_local * dest + head) * head_dim
            x = part_refs[parts.index(part)][:, :, :, at : at + head_dim].astype(jnp.float32)
            if part in gains:
                meansq = jnp.mean(x * x, axis=-1, keepdims=True)
                x = x * lax.rsqrt(meansq + 1e-06) * gains[part]
            x = x.reshape(frames, rows * cols, head_dim).astype(jnp.bfloat16)
            out_ref[dest, slot * frames : (slot + 1) * frames] = x
            if tiles:
                rim_refs[0][dest, slot * TT : (slot + 1) * TT] = x[:TT]
                rim_refs[1][dest, slot * TT : (slot + 1) * TT] = x[frames - TT :]


def whole(shape):
    return pl.BlockSpec(shape, lambda i: (0,) * len(shape))


def one_step(kernel, in_specs, outs, size, grant=None):
    shapes = [jax.ShapeDtypeStruct(shape, jnp.bfloat16) for shape in outs]
    return pl.pallas_call(
        kernel,
        grid=(1,),
        in_specs=in_specs,
        out_specs=[whole(shape) for shape in outs],
        out_shape=shapes,
        cost_estimate=cost(size, size),
        compiler_params=pltpu.CompilerParams(vmem_limit_bytes=grant or GRANT),
    )


def pack(qkv, q_gain, k_gain, entries, heads_local, groups, tiles=False):
    frames, rows, cols, channels = qkv.shape
    head_dim = q_gain.shape[-1]
    third = channels // 3
    parts = sorted({part for part, _ in entries})
    n = len(entries)
    own = rows * cols
    outs = [(groups, n * frames, own, head_dim)] + [(groups, n * TT, own, head_dim)] * (2 * tiles)
    in_specs = [
        pl.BlockSpec((frames, rows, cols, third), functools.partial(lambda p, i: (0, 0, 0, p), part))
        for part in parts
    ] + [whole((1, head_dim))] * 2
    kernel = functools.partial(pack_kernel, entries, parts, heads_local, tiles)
    packed = one_step(kernel, in_specs, outs, 4 * math.prod(outs[0]), PACK_GRANT)(
        *([qkv] * len(parts)), q_gain.reshape(1, -1), k_gain.reshape(1, -1)
    )
    return packed if tiles else packed[0]


def join_kernel(frames, c_ref, t0_ref, t1_ref, out_ref):
    long = frames + 2 * TT
    for kv in range(2):
        at = kv * long
        out_ref[:, at : at + TT] = t0_ref[:, kv * TT : (kv + 1) * TT]
        out_ref[:, at + TT : at + TT + frames] = c_ref[:, kv * frames : (kv + 1) * frames]
        out_ref[:, at + TT + frames : at + long] = t1_ref[:, kv * TT : (kv + 1) * TT]


def join(center, t0, t1):
    groups, slabs, own, head_dim = center.shape
    frames = slabs // 2
    total = 2 * (frames + 2 * TT)
    arrays = (center, t0, t1)
    out = (groups, total, own, head_dim)
    return one_step(
        functools.partial(join_kernel, frames),
        [whole(a.shape) for a in arrays],
        [out],
        4 * math.prod(out),
        PACK_GRANT,
    )(*arrays)[0]


def tiles_kernel(frames, ref, first_ref, last_ref):
    for n in range(ref.shape[1] // frames):
        to = slice(n * TT, (n + 1) * TT)
        first_ref[:, to] = ref[:, n * frames : n * frames + TT]
        last_ref[:, to] = ref[:, (n + 1) * frames - TT : (n + 1) * frames]


def tiles_of(value, frames):
    groups, slabs, own, head_dim = value.shape
    out = (groups, slabs // frames * TT, own, head_dim)
    return one_step(
        functools.partial(tiles_kernel, frames),
        [whole(value.shape)],
        [out, out],
        8 * math.prod(out),
    )(value)


def rim_kernel(edge, counts, *refs):
    low_ref, high_ref = refs[-2:]
    sources = refs[:-2]
    own = sources[0].shape[2]
    total = sum(counts)
    for n in range(low_ref.shape[1] // total):
        at = n * total
        for ref, count in zip(sources, counts):
            src = slice(n * count, (n + 1) * count)
            low_ref[:, at : at + count] = ref[:, src, 0:edge]
            high_ref[:, at : at + count] = ref[:, src, own - edge : own]
            at += count


def rim(arrays, counts, heads, edge):
    groups, _, own, head_dim = arrays[0].shape
    out = (groups, heads * sum(counts), edge, head_dim)
    in_specs = [whole((groups, heads * c, own, head_dim)) for c in counts]
    return one_step(
        functools.partial(rim_kernel, edge, counts), in_specs, [out, out], 8 * math.prod(out)
    )(*arrays)


def attend_kernel(pieces, frames, span, reach, scale, head, slot, info_ref, *refs):
    count = len(pieces)
    piece_refs = refs[:count]
    q_ref = refs[count]
    out_ref, k_ref, v_ref, bias_ref = refs[-4:]
    here = slot + pl.program_id(0)
    if len(refs) > count + 5:
        out_ref[:, 0:slot] = refs[count + 1][...]
    groups = q_ref.shape[0]
    own, head_dim = q_ref.shape[2:]
    edge = TH * TW
    for ref, (spans, low) in zip(piece_refs, pieces):
        tokens = slice(low, low + ref.shape[2])
        at = 0
        for dst in (k_ref, v_ref):
            for start, n in spans:
                dst[:, start : start + n, tokens] = ref[:, at : at + n]
                at += n

    tiles_t = frames // TT
    tiles_h = own // edge
    base_t = info_ref.shape[0] - (tiles_t + 2) - (tiles_h + 2)
    base_h = base_t + tiles_t + 2
    head = head + pl.program_id(0)
    rad_t = info_ref[3 * head]
    rad_h = info_ref[3 * head + 1]
    rad_w = info_ref[3 * head + 2]
    nq = span * TT * edge
    at_q = lax.broadcasted_iota(jnp.int32, (nq, 1), 0) % (TT * edge)
    q_frame = at_q // edge
    q_row = (at_q % edge) // TW
    firsts = [min(max(half * span - 1, 0), groups - reach) for half in range(groups // span)]

    def over(far_t, far_h):
        near_t = 1 + 2 * far_t
        near_h = 1 + 2 * far_h
        per_col = near_t * TT * near_h * edge
        nk = reach * per_col
        q_col = lax.broadcasted_iota(jnp.int32, (nq, nk), 0) // (TT * edge)
        k_col = lax.broadcasted_iota(jnp.int32, (nq, nk), 1) // per_col
        for half, first in enumerate(firsts):
            gap = jnp.abs(q_col - k_col + (half * span - first))
            bias_ref[half, :, :nk] = jnp.where(gap <= rad_w, 0.0, NEG)
        at = lax.broadcasted_iota(jnp.int32, (1, nk), 1) % per_col
        k_frame = at // (near_h * edge)
        k_row = (at % (near_h * edge)) // TW

        @pl.loop(0, tiles_t * tiles_h)
        def _(step):
            th = step % tiles_h
            tt = step // tiles_h
            live_t = jnp.zeros((1, nk), jnp.int32)
            live_h = jnp.zeros((1, nk), jnp.int32)
            for near in range(near_t):
                count = info_ref[base_t + tt + 1 - far_t + near]
                live_t = jnp.where(k_frame // TT == near, count, live_t)
            for near in range(near_h):
                count = info_ref[base_h + th + 1 - far_h + near]
                live_h = jnp.where(k_row // TH == near, count, live_h)
            key_ok = (k_frame % TT < live_t) & (k_row % TH < live_h)
            key_bias = jnp.where(key_ok, 0.0, NEG)
            live = (q_frame < info_ref[base_t + tt + 1]) & (q_row < info_ref[base_h + th + 1])
            q_rows = pl.ds(pl.multiple_of(th * edge, edge), edge)
            k_rows = pl.ds(pl.multiple_of((th + 1 - far_h) * edge, edge), near_h * edge)
            q_frames = pl.ds(tt * TT, TT)
            k_frames = pl.ds((tt + 1 - far_t) * TT, near_t * TT)
            for half, first in enumerate(firsts):
                q_cols = slice(half * span, (half + 1) * span)
                k_cols = slice(first, first + reach)
                q = q_ref[q_cols, q_frames, q_rows, :].reshape(nq, head_dim)
                k = k_ref[k_cols, k_frames, k_rows, :].reshape(nk, head_dim)
                v = v_ref[k_cols, k_frames, k_rows, :].reshape(nk, head_dim)
                scores = lax.dot_general(
                    q, k, (((1,), (1,)), ((), ())), preferred_element_type=jnp.float32
                )
                scores = scores * scale + (bias_ref[half, :, :nk] + key_bias)
                top = jnp.max(scores, axis=1, keepdims=True)
                raised = jnp.exp2(scores - top)
                summed = jnp.sum(raised, axis=1, keepdims=True)
                blended = jnp.dot(
                    raised.astype(jnp.bfloat16), v, preferred_element_type=jnp.float32
                )
                result = jnp.where(live, blended / summed, 0.0).astype(jnp.bfloat16)
                out_ref[q_cols, here, q_frames, q_rows, :] = result.reshape(
                    span, TT, edge, head_dim
                )

    for far_t in (0, 1):
        for far_h in (0, 1):
            pl.when((rad_t == far_t) & (rad_h == far_h))(functools.partial(over, far_t, far_h))


def attend(info, pieces, queries, heads, head, slot, before, frames):
    groups, _, own, head_dim = queries.shape
    span = max(groups // 2, 1)
    reach = min(span + 1, groups)
    edge = TH * TW
    nq = span * TT * edge
    nk = reach * 9 * TT * edge
    steps = heads * (frames // TT) * (own // edge) * (groups // span)
    ext = (groups, frames + 2 * TT, own + 2 * edge, head_dim)
    in_specs = [pl.BlockSpec(memory_space=pltpu.SMEM)]
    in_specs += [
        pl.BlockSpec(
            (groups, 2 * sum(n for _, n in spans), a.shape[2], head_dim), lambda h: (0, h, 0, 0)
        )
        for a, spans, _ in pieces
    ]
    in_specs += [
        pl.BlockSpec((groups, frames, own, head_dim), lambda h: (0, head + h, 0, 0)),
    ]
    args = [info, *(a for a, _, _ in pieces), queries]
    total = slot + heads
    if before is not None:
        in_specs.append(pl.BlockSpec(before.shape, lambda h: (0, 0, 0, 0, 0)))
        args.append(before)
    return pl.pallas_call(
        functools.partial(
            attend_kernel,
            tuple((spans, low) for _, spans, low in pieces),
            frames,
            span,
            reach,
            math.log2(math.e) / math.sqrt(head_dim),
            head,
            slot,
        ),
        grid=(heads,),
        in_specs=in_specs,
        out_specs=pl.BlockSpec(memory_space=pltpu.VMEM),
        out_shape=pltpu.VMEM((groups, total, frames, own, head_dim), jnp.bfloat16),
        scratch_shapes=[
            pltpu.VMEM(ext, jnp.bfloat16),
            pltpu.VMEM(ext, jnp.bfloat16),
            pltpu.VMEM((groups // span, nq, nk), jnp.float32),
        ],
        cost_estimate=cost(4 * steps * nq * nk * head_dim, heads * (4 << 20), steps * nq * nk),
        compiler_params=pltpu.CompilerParams(vmem_limit_bytes=GRANT),
        name="attend",
    )(*args)


def unpack_kernel(order, *refs):
    out_ref = refs[-1]
    frames, rows, cols = out_ref.shape[:3]
    heads = len(order)
    slots = [(ref, slot) for ref in refs[:-1] for slot in range(ref.shape[1])]
    for (ref, slot), head in zip(slots, order):
        groups, _, _, _, head_dim = ref.shape
        for group in range(groups):
            at = (heads * group + head) * head_dim
            x = ref[group, slot].astype(jnp.float32).reshape(frames, rows, cols, head_dim)
            out_ref[:, :, :, at : at + head_dim] = x.astype(jnp.bfloat16)


def unpack(values, order, rows, cols):
    groups, _, frames, _, head_dim = values[0].shape
    out = (frames, rows, cols, groups * len(order) * head_dim)
    return pl.pallas_call(
        functools.partial(unpack_kernel, order),
        in_specs=[pl.BlockSpec(memory_space=pltpu.VMEM)] * len(values),
        out_specs=pl.BlockSpec(memory_space=pltpu.VMEM),
        out_shape=jax.ShapeDtypeStruct(out, jnp.bfloat16),
        compiler_params=pltpu.CompilerParams(vmem_limit_bytes=16 << 20),
        name="unpack",
    )(*values)


def shifted(value, axis, step):
    size = lax.axis_size(axis)
    pairs = [(i, i + 1) if step > 0 else (i + 1, i) for i in range(size - 1)]
    return lax.ppermute(value, axis, pairs)


def exchange(value):
    return lax.all_to_all(value, "hd", split_axis=0, concat_axis=0, tiled=True)


def shards(qkv, q_gain, k_gain, windows, frame_counts, row_counts):
    frames, rows, cols, channels = qkv.shape
    head_dim = q_gain.shape[0]
    groups = lax.axis_size("hd")
    heads = channels // (3 * head_dim) // groups
    edge = TH * TW
    own = rows * cols
    tiles_t = frames // TT
    tiles_h = rows // TH
    near_t = lax.dynamic_slice(
        jnp.pad(frame_counts, (1, 1)), (lax.axis_index("ta") * tiles_t,), (tiles_t + 2,)
    )
    near_h = lax.dynamic_slice(
        jnp.pad(row_counts, (1, 1)), (lax.axis_index("ha") * tiles_h,), (tiles_h + 2,)
    )
    info = jnp.concatenate([windows.reshape(-1), near_t, near_h])

    def packed(entries, tiles=False):
        return pack(qkv, q_gain, k_gain, tuple(entries), heads, groups, tiles)

    rest = heads - 1
    long = frames + 2 * TT
    value_z, first_z, last_z = packed([(1, rest), (2, rest)], True)
    tz0 = shifted(last_z, "ta", 1)
    tz1 = shifted(first_z, "ta", -1)
    value_n = packed([(part, head) for head in range(rest) for part in (1, 2)])
    got_n = exchange(value_n)
    got_q = exchange(packed([(0, head) for head in range(heads)]))
    joined = join(value_z, tz0, tz1)
    got_z = exchange(joined)

    first_n, last_n = tiles_of(got_n, frames)
    tn0 = shifted(last_n, "ta", 1)
    tn1 = shifted(first_n, "ta", -1)
    low_c, high_c = rim((got_n,), (frames,), 2 * rest, edge)
    hc0 = shifted(high_c, "ha", 1)
    hc1 = shifted(low_c, "ha", -1)
    low_z, high_z = rim((got_z,), (long,), 2, edge)
    hz0 = shifted(high_z, "ha", 1)
    hz1 = shifted(low_z, "ha", -1)
    low_t, high_t = rim((tn0, tn1), (TT, TT), 2 * rest, edge)
    ht0 = shifted(high_t, "ha", 1)
    ht1 = shifted(low_t, "ha", -1)

    mine, every = ((TT, frames),), ((0, long),)
    beside = ((0, TT), (TT + frames, TT))
    pieces_n = (
        (got_n, mine, edge),
        (tn0, ((0, TT),), edge),
        (tn1, ((TT + frames, TT),), edge),
        (hc0, mine, 0),
        (hc1, mine, edge + own),
        (ht0, beside, 0),
        (ht1, beside, edge + own),
    )
    pieces_z = ((got_z, every, edge), (hz0, every, 0), (hz1, every, edge + own))
    out_z = attend(info, pieces_z, got_q, 1, rest, 0, None, frames)
    back_z = exchange(out_z)
    out_n = attend(info, pieces_n, got_q, rest, 0, 0, None, frames)
    return unpack((back_z, exchange(out_n)), (rest, *range(rest)), rows, cols)


def solution(mesh):
    return jax.shard_map(
        shards,
        mesh=mesh,
        in_specs=(P("ta", "ha", "hd", None), P(), P(), P("hd", None), P(), P()),
        out_specs=P("ta", "ha", "hd", None),
        check_vma=False,
    )
```
